32 devices in a mesh: groups: 2 (over y), seq: 16 (over z, x, core).
Axes of the slice: x: 2, y: 2, z: 4, core: 2. Of those that a mesh axis runs over, the one named last changes fastest.
Arguments:
- inputs: bfloat16 [4, 8192, 1536], P('groups', 'seq'), parts along dimension 0, may hold values from -6 to 6
- conv_weight: bfloat16 [3, 1536, 768], P(None, 'seq'), may hold values from -0.09375 to 0.09375
- proj_weight: bfloat16 [1536, 768], P('seq'), may hold values from -0.21875 to 0.21875
- cotangent: bfloat16 [4, 8192, 1536], P('groups', 'seq'), parts along dimension 0, may hold values from -6 to 6
Outputs:
- outputs: bfloat16 [4, 8192, 1536], P('groups', 'seq'), parts along dimension 0
- input_grad: bfloat16 [4, 8192, 1536], P('groups', 'seq'), parts along dimension 0
- conv_grad: float32 [3072, 3, 768], P(('groups', 'seq')), parts along dimension 0
- proj_grad: float32 [3072, 768], P(('groups', 'seq')), parts along dimension 0
The draws below stay inside these ranges and needn't reach their ends.
There are 2 independent parts, one for each index of `groups`. The reference program is written for one: setup_inputs(seed, part) draws one part's arguments, and reference() takes and returns one part's arrays. A program takes and returns all parts, laid end to end along the dimension named above; an argument that names none is the same for every part. Nothing has to cross between parts.
All inputs are finite; a program needn't handle non-finite values.
Results may differ from the reference program's by a relative error of at most 0.0051.
Values may be sent and summed in bfloat16 or wider, within the bound.
A program may use at most 128 MiB of HBM per device.

```python
import jax
import jax.numpy as jnp

C = 1536
H = 768
L = 8192
B = 2


def spiked(array, stream_key, source, target, blocks, factor):
    def block_of(dim):
        return (jnp.arange(array.shape[dim]) // (array.shape[dim] // blocks)).reshape((-1,) + (1,) * (array.ndim - 1 - dim))

    first = jax.random.permutation(stream_key, blocks)[block_of(target)]
    far = (block_of(target) + blocks // 2) % blocks
    return jnp.where((block_of(source) == first) | (block_of(source) == far), factor * array, array)


def block_scale(own_key, shape, pieces, least, high):
    def one(dim, blocks):
        heights = jax.random.uniform(jax.random.fold_in(jax.random.fold_in(own_key, 6), dim), (blocks,), jnp.float32, least / len(pieces), high / len(pieces))
        return jnp.repeat(jnp.exp(heights), shape[dim] // blocks).reshape((-1,) + (1,) * (len(shape) - dim - 1))

    gain = one(*pieces[0])
    for cut in pieces[1:]:
        gain = gain * one(*cut)
    return gain


def normal_values(stream_key, extent, spread, limit, pieces=(), kind=jnp.bfloat16):
    level = block_scale(stream_key, extent, pieces, -0.22, 0.18) if pieces else 1.0
    result = jax.random.normal(stream_key, extent, jnp.float32) * spread * level
    return jnp.minimum(jnp.maximum(result, -limit), limit).astype(kind)


def heavy_noise(rng, extent, deviation, bound, pieces, heavy, dtype=jnp.bfloat16):
    array = deviation * jax.random.normal(rng, extent, jnp.float32)
    if pieces:
        array = array * block_scale(rng, extent, pieces, -0.22, 0.18)
    return jnp.clip(spiked(array, jax.random.fold_in(rng, 3), *heavy), -bound, bound).astype(dtype)


def setup_inputs(seed: int = 0, part: int = 0) -> dict:
    arg_keys = jax.random.split(jax.random.key(seed), 5)
    own_keys = jax.random.split(jax.random.fold_in(arg_keys[4], part), 5)
    return {
        "inputs": heavy_noise(own_keys[0], (B, L, C), 1.0, 6.0, ((1, 16),), (1, 2, 16, 2.0)),
        "conv_weight": normal_values(arg_keys[1], (3, C, H), (3 * C) ** -0.5, 0.09375, ((1, 16),)),
        "proj_weight": normal_values(arg_keys[2], (C, H), H ** -0.5, 0.21875, ((0, 16),)),
        "cotangent": heavy_noise(own_keys[3], (B, L, C), 1.0, 6.0, ((1, 16),), (1, 2, 16, 2.0)),
    }


def shift_rows(values, offset):
    width = values.shape[1]
    if offset > 0:
        padded = jnp.pad(values, ((0, 0), (0, offset), (0, 0)))
        return padded[:, offset:offset + width, :]
    if offset < 0:
        padded = jnp.pad(values, ((0, 0), (-offset, 0), (0, 0)))
        return padded[:, :width, :]
    return values

def gelu_grad(point, upstream):
    return jax.vjp(jax.nn.gelu, point)[1](upstream)[0]

def reference(inputs, conv_weight, proj_weight, cotangent):
    dilation = L // 8
    batch = inputs.shape[0]
    chans = inputs.shape[2]
    hid = conv_weight.shape[2]
    scale = 1.0 / float(batch * L) ** 0.5
    acted = jax.nn.gelu(inputs.astype(jnp.float32)).astype(jnp.bfloat16)
    hidden = jnp.zeros((batch * L, hid), jnp.float32)
    for k in range(3):
        moved = shift_rows(acted, (k - 1) * dilation).reshape(-1, chans)
        hidden = hidden + jnp.dot(moved, conv_weight[k], preferred_element_type=jnp.float32)
    gated = jax.nn.gelu(hidden).astype(jnp.bfloat16)
    outputs = (inputs.reshape(-1, chans).astype(jnp.float32) + jnp.dot(gated, proj_weight.T, preferred_element_type=jnp.float32)).astype(jnp.bfloat16)
    cot_rows = cotangent.reshape(-1, chans)
    gated_grad = jnp.dot(cot_rows, proj_weight, preferred_element_type=jnp.float32)
    hidden_grad = gelu_grad(hidden, gated_grad).astype(jnp.bfloat16)
    grad_blocks = hidden_grad.reshape(batch, L, hid)
    acted_grad = jnp.zeros((batch * L, chans), jnp.float32)
    kernel_parts = []
    for k in range(3):
        moved_grad = shift_rows(grad_blocks, -(k - 1) * dilation).reshape(-1, hid)
        acted_grad = acted_grad + jnp.dot(moved_grad, conv_weight[k].T, preferred_element_type=jnp.float32)
        moved = shift_rows(acted, (k - 1) * dilation).reshape(-1, chans)
        kernel_parts.append(jnp.dot(moved.T, hidden_grad, preferred_element_type=jnp.float32))
    input_grad = (cot_rows.astype(jnp.float32) + gelu_grad(inputs.reshape(-1, chans).astype(jnp.float32), acted_grad)).astype(jnp.bfloat16)
    conv_grad = jnp.stack(kernel_parts, axis=1) * scale
    proj_grad = jnp.dot(cot_rows.T, gated, preferred_element_type=jnp.float32) * scale
    return (outputs.reshape(batch, L, chans), input_grad.reshape(batch, L, chans), conv_grad, proj_grad)
```

```python
import functools

import jax
import jax.numpy as jnp
from jax import lax
from jax.experimental import pallas as pl
from jax.experimental.pallas import tpu as pltpu
from jax.sharding import PartitionSpec as P

L = 8192


def from_behind(block, axis, distance):
    devices = range(lax.axis_size(axis))
    route = [(i - distance, i) for i in devices if i - distance in devices]
    return lax.ppermute(block, axis, route)


def gelu_grad(point, upstream):
    return jax.vjp(jax.nn.gelu, point)[1](upstream)[0]


def shards(inputs, conv_weight, proj_weight, cotangent):
    batch, local_len, chans = inputs.shape
    devices = lax.axis_size("seq")
    stride = devices // 8
    scale = 1.0 / float(batch * L) ** 0.5
    acted = jax.nn.gelu(inputs.astype(jnp.float32)).astype(jnp.bfloat16)
    conv_weight, proj_weight = (
        lax.all_gather(conv_weight, "seq", axis=1, tiled=True),
        lax.all_gather(proj_weight, "seq", axis=0, tiled=True),
    )
    hid = conv_weight.shape[2]
    acted_rows = acted.reshape(-1, chans)
    before = from_behind(acted, "seq", stride)
    after = from_behind(acted, "seq", -stride)
    hidden = jnp.dot(before.reshape(-1, chans), conv_weight[0], preferred_element_type=jnp.float32)
    hidden = hidden + jnp.dot(acted_rows, conv_weight[1], preferred_element_type=jnp.float32)
    hidden = hidden + jnp.dot(
        after.reshape(-1, chans), conv_weight[2], preferred_element_type=jnp.float32
    )
    gated = jax.nn.gelu(hidden).astype(jnp.bfloat16)
    outputs = (
        inputs.reshape(-1, chans).astype(jnp.float32)
        + jnp.dot(gated, proj_weight.T, preferred_element_type=jnp.float32)
    ).astype(jnp.bfloat16)
    cot_rows = cotangent.reshape(-1, chans)
    gated_grad = jnp.dot(cot_rows, proj_weight, preferred_element_type=jnp.float32)
    hidden_grad = gelu_grad(hidden, gated_grad).astype(jnp.bfloat16)
    grad_blocks = hidden_grad.reshape(batch, local_len, hid)
    grad_later = from_behind(grad_blocks, "seq", -stride).reshape(-1, hid)
    grad_earlier = from_behind(grad_blocks, "seq", stride).reshape(-1, hid)
    acted_grad = jnp.dot(grad_later, conv_weight[0].T, preferred_element_type=jnp.float32)
    acted_grad = acted_grad + jnp.dot(
        hidden_grad, conv_weight[1].T, preferred_element_type=jnp.float32
    )
    acted_grad = acted_grad + jnp.dot(
        grad_earlier, conv_weight[2].T, preferred_element_type=jnp.float32
    )
    input_grad = (
        cot_rows.astype(jnp.float32)
        + gelu_grad(inputs.reshape(-1, chans).astype(jnp.float32), acted_grad)
    ).astype(jnp.bfloat16)
    tap_grads = (grad_later, hidden_grad, grad_earlier)
    share = chans // devices
    local_terms = [
        jnp.dot(acted_rows.T, piece, preferred_element_type=jnp.float32) for piece in tap_grads
    ]
    local_terms.append(jnp.dot(cot_rows.T, gated, preferred_element_type=jnp.float32))
    stacked = jnp.stack(local_terms, axis=1)
    received = lax.all_to_all(stacked, "seq", split_axis=0, concat_axis=0, tiled=True)
    summed = jnp.sum(received.reshape(devices, share, 4, received.shape[2]), axis=0)
    conv_sum = summed[:, 0:3, :]
    proj_sum = summed[:, 3, :]
    return (
        outputs.reshape(batch, local_len, chans),
        input_grad.reshape(batch, local_len, chans),
        conv_sum * scale,
        proj_sum * scale,
    )


F32 = jnp.float32
BF16 = jnp.bfloat16
MESH = pl.DeviceIdType.MESH
VMEM = pl.BlockSpec(memory_space=pltpu.VMEM)
HBM = pl.BlockSpec(memory_space=pl.ANY)
SEQ = 16
CHUNKS = 4
HALO = 8
COEF = 0.7978845608028654
CUBE = 0.044715


def place():
    s = lax.axis_index("seq")
    return s // 4, (s // 2) % 2, s % 2


def index(z, x, core):
    return (z * 2 + x) * 2 + core


def copy_to(src, dst, send, recv, target):
    return pltpu.make_async_remote_copy(
        src_ref=src, dst_ref=dst, send_sem=send, recv_sem=recv,
        device_id={"seq": target}, device_id_type=MESH,
    )


def greet(targets):
    barrier = pltpu.get_barrier_semaphore()
    for target in targets:
        pl.semaphore_signal(barrier, inc=1, device_id={"seq": target}, device_id_type=MESH)
    pl.semaphore_wait(barrier, len(targets))


def gelu_parts(v):
    t = jnp.tanh(COEF * (v + CUBE * v * v * v))
    half = 0.5 * (1.0 + t)
    return half * v, half + (0.5 * COEF) * v * (1.0 - t * t) * (1.0 + (3.0 * CUBE) * v * v)


def params(cid, mib=56):
    return pltpu.CompilerParams(
        collective_id=cid, has_side_effects=True, vmem_limit_bytes=mib * 1024 * 1024
    )


def forward_kernel(conv_hbm, proj_hbm, x_hbm, cot_hbm, full_hbm, acted_hbm, gated_ref, hg_ref,
                   w_buf, x_ref, cot_ref, acted_ref, out_a, in_a, out_s, in_s, part, gg, own_sem,
                   zs, zr, xs, xr, ys, yr, cs, cr, os, orv,
                   hzs, hzr, hxs, hxr):
    z, x, core = place()
    group = lax.axis_index("groups")
    me = lax.axis_index("seq")
    share = proj_hbm.shape[0]
    across = index(z, 1 - x, core)
    other = index(z, x, 1 - core)
    origin = (z + 1 - 2 * lax.rem(z, 2), 2 - z // 2, 3 - 3 * (z // 2), z)
    up = x == 1
    sends = jnp.logical_or(jnp.logical_and(up, z < 3), jnp.logical_and(x == 0, z > 0))
    takes = jnp.logical_or(jnp.logical_and(up, z > 0), jnp.logical_and(x == 0, z < 3))
    ahead = index(lax.rem(z + (2 * x - 1) + 4, 4), x, core)

    mine = pl.ds(pl.multiple_of(me * share, share), share)
    loads = [
        pltpu.make_async_copy(conv_hbm.at[tap], w_buf.at[slot, mine, :], own_sem.at[slot])
        for slot, tap in enumerate((0, 2, 1))
    ]
    loads.append(pltpu.make_async_copy(proj_hbm, w_buf.at[3, mine, :], own_sem.at[3]))
    x_load = pltpu.make_async_copy(x_hbm, x_ref, own_sem.at[4])
    cot_load = pltpu.make_async_copy(cot_hbm, cot_ref, own_sem.at[5])
    for load in loads:
        load.start()
    x_load.start()
    cot_load.start()
    barrier = pltpu.get_barrier_semaphore()
    for target in [index(origin[j], x, core) for j in range(3)] + [across, other]:
        pl.semaphore_signal(barrier, inc=1, device_id={"seq": target}, device_id_type=MESH)
    pl.semaphore_signal(
        barrier, inc=1, device_id={"groups": 1 - group, "seq": me}, device_id_type=MESH
    )
    pl.semaphore_wait(barrier, 6)

    slots = (1 - x, x, 2, 3)
    half = share // 2

    def piece(p, j, xx, start, size):
        begin = pl.multiple_of(index(origin[j], xx, core) * share + start, 16)
        return w_buf.at[slots[p], pl.ds(begin, size), :]

    def plane(p, j, xx):
        return piece(p, j, xx, group * half, half)

    def z_copy(q, d):
        place_ = plane((0, 0, 2, 3)[q], 3, 1 - x if q == 1 else x)
        return copy_to(place_, place_, zs.at[q, d], zr.at[q, z], index(origin[d], x, core))

    def z_came(q, j):
        place_ = plane((0, 0, 2, 3)[q], j, 1 - x if q == 1 else x)
        copy_to(place_, place_, zs.at[q, 0], zr.at[q, origin[j]], across).wait_recv()

    def z_begin(q):
        for d in range(3):
            z_copy(q, d).start()

    def x_copy(p, j):
        place_ = plane(1 - p if p < 2 else p, j % 4, x if j < 4 else 1 - x)
        return copy_to(place_, place_, xs.at[p, j], xr.at[p, j], across)

    def x_came(p, j):
        place_ = plane(p, j % 4, 1 - x if j < 4 else x)
        copy_to(place_, place_, xs.at[p, j], xr.at[p, j], across).wait_recv()

    def column(j):
        return j % 4, (x if j < 4 else 1 - x)

    def y_copy(p, j, whose):
        place_ = piece(p, *column(j), whose * half, half)
        return pltpu.make_async_remote_copy(
            src_ref=place_, dst_ref=place_, send_sem=ys.at[p, j], recv_sem=yr.at[p, j],
            device_id={"groups": 1 - group, "seq": me}, device_id_type=MESH,
        )

    def core_copy(p, j):
        place_ = piece(p, *column(j), 0, share)
        return copy_to(place_, place_, cs.at[p, j], cr.at[p, j], other)

    def own_core():
        place_ = w_buf.at[:, mine, :]
        return copy_to(place_, place_, os.at[0], orv.at[0], other)

    def own_core_came():
        start = pl.multiple_of(other * share, 16)
        place_ = w_buf.at[:, pl.ds(start, share), :]
        copy_to(place_, place_, os.at[0], orv.at[0], other).wait_recv()

    def take_z(q, j):
        z_came(q, j)
        p = (0, 0, 2, 3)[q]
        y_copy(p, j + 4 if q == 1 else j, group).start()
        x_copy(1 if q < 2 else q, j + 4 if q == 1 else j).start()

    def take_x(p, j):
        x_came(p, j)
        y_copy(p, j + 4 if j < 4 else j - 4, group).start()

    def take_y(p, j):
        y_copy(p, j, 1 - group).wait_recv()
        core_copy(p, j).start()

    def core_came(p):
        for j in swapped:
            place_ = w_buf.at[
                slots[p],
                pl.ds(pl.multiple_of(index(origin[j % 4], x if j < 4 else 1 - x, 1 - core) * share, 16), share),
                :,
            ]
            copy_to(place_, place_, cs.at[p, j], cr.at[p, j], other).wait_recv()

    swapped = (0, 1, 2, 4, 5, 6, 7)
    x_sent = ((0, 3),) + tuple((1, j) for j in range(7)) + tuple((p, j) for p in (2, 3) for j in range(4))
    m = acted_ref.shape[0]
    n = m // CHUNKS
    h = m // HALO

    def rows(i):
        return pl.ds(pl.multiple_of(i * n, n), n)

    def part_rows(i):
        return pl.ds(pl.multiple_of(i * h, h), h)

    def halo_z(i):
        r = part_rows(i)
        return copy_to(out_a.at[r, :], in_a.at[r, :], hzs.at[i], hzr.at[i], ahead)

    def halo_x(i):
        r = part_rows(i)
        return copy_to(out_s.at[r, :], in_s.at[r, :], hxs.at[i], hxr.at[i], across)

    tile = 64

    def act(i, carry):
        r = pl.ds(pl.multiple_of(i * tile, tile), tile)
        v = x_ref[r, :].astype(F32)
        t = jnp.tanh(COEF * (v + CUBE * v * v * v))
        acted_ref[r, :] = (0.5 * v * (1.0 + t)).astype(BF16)
        return carry

    def far_part(i, carry):
        out_a[rows(i), :] = jnp.dot(
            acted_ref[rows(i), :], w_buf[1 - x], preferred_element_type=F32
        ).astype(BF16)

        @pl.when(sends)
        def _():
            for k in range(HALO // CHUNKS):
                halo_z(i * (HALO // CHUNKS) + k).start()
        return carry

    def near_part(i, carry):
        part[rows(i), :] = jnp.dot(acted_ref[rows(i), :], w_buf[x], preferred_element_type=F32)
        return carry

    def combine(i):
        r = part_rows(i)

        @pl.when(takes)
        def _():
            halo_z(i).wait_recv()
            part[r, :] = part[r, :] + in_a[r, :].astype(F32)
        out_s[r, :] = part[r, :].astype(BF16)
        halo_x(i).start()

    def middle(i, carry):
        part[rows(i), :] = jnp.dot(acted_ref[rows(i), :], w_buf[2], preferred_element_type=F32)
        gg[rows(i), :] = jnp.dot(cot_ref[rows(i), :], w_buf[3], preferred_element_type=F32)
        return carry

    def finish(i, carry):
        r = part_rows(i)
        halo_x(i).wait_recv()
        hidden = part[r, :] + in_s[r, :].astype(F32)
        value, slope = gelu_parts(hidden)
        gated_ref[r, :] = value.astype(BF16)
        hg_ref[r, :] = (gg[r, :] * slope).astype(BF16)
        return carry

    for load in loads:
        load.wait()
    z_begin(0)
    x_copy(0, 3).start()
    x_copy(1, 3).start()
    own_core().start()
    x_load.wait()
    steps = m // tile
    lax.fori_loop(0, steps // 2, act, 0)
    take_x(0, 3)
    z_begin(1)
    lax.fori_loop(steps // 2, steps, act, 0)
    acted_store = pltpu.make_async_copy(acted_ref, acted_hbm, own_sem.at[6])
    acted_store.start()
    take_z(0, 0)
    take_z(0, 1)
    take_x(1, 3)
    take_z(0, 2)
    z_begin(2)
    x_copy(2, 3).start()
    x_copy(3, 3).start()
    take_x(1, 0)
    take_z(1, 0)
    take_x(1, 1)
    take_y(0, 7)
    take_z(1, 1)
    take_y(0, 0)
    take_y(0, 1)
    take_z(1, 2)
    z_begin(3)
    take_x(1, 2)
    take_y(0, 2)
    take_x(1, 4)
    take_x(1, 5)
    take_y(0, 4)
    take_y(0, 5)
    take_x(1, 6)
    take_y(0, 6)
    own_core_came()
    core_came(0)
    lax.fori_loop(0, CHUNKS, far_part, 0)
    take_z(2, 0)
    take_x(2, 3)
    take_x(3, 3)
    for j in (7, 4, 5, 6):
        take_y(1, j)
    take_z(2, 1)
    take_x(2, 0)
    take_z(2, 2)
    take_x(2, 1)
    take_x(2, 2)
    for j in (0, 1, 2):
        take_y(1, j)
    core_came(1)
    lax.fori_loop(0, CHUNKS, near_part, 0)
    combine(0)
    for j in range(3):
        take_z(3, j)
    take_x(3, 0)
    combine(1)
    take_x(3, 1)
    take_x(3, 2)
    combine(2)
    for j in (0, 7, 1, 4):
        take_y(2, j)
    combine(3)
    for j in (2, 5, 6):
        take_y(2, j)
    combine(4)
    for j in (7, 0, 1, 4):
        take_y(3, j)
    combine(5)
    for j in (2, 5, 6):
        take_y(3, j)
    combine(6)
    core_came(2)
    core_came(3)
    cot_load.wait()
    keep = pltpu.make_async_copy(w_buf, full_hbm, own_sem.at[7])
    keep.start()
    lax.fori_loop(0, CHUNKS - 1, middle, 0)
    combine(7)
    lax.fori_loop(CHUNKS - 1, CHUNKS, middle, 0)
    lax.fori_loop(0, HALO, finish, 0)
    own_core().wait_send()
    for q in range(4):
        for d in range(3):
            z_copy(q, d).wait_send()
    for p, j in x_sent:
        x_copy(p, j).wait_send()
    for p in range(4):
        for j in swapped:
            y_copy(p, j, group).wait_send()
            core_copy(p, j).wait_send()
    for i in range(HALO):
        halo_x(i).wait_send()

    @pl.when(sends)
    def _():
        for i in range(HALO):
            halo_z(i).wait_send()

    keep.wait()
    acted_store.wait()


def forward(conv_weight, proj_weight, flat, cot):
    taps, share, hid = 4, proj_weight.shape[0], proj_weight.shape[1]
    m = flat.shape[0]
    dma = pltpu.SemaphoreType.DMA
    full = jax.ShapeDtypeStruct((taps, share * SEQ, hid), BF16)
    return pl.pallas_call(
        forward_kernel,
        out_shape=(full, jax.ShapeDtypeStruct(flat.shape, BF16))
        + (jax.ShapeDtypeStruct((m, hid), BF16),) * 2,
        in_specs=[HBM] * 4,
        out_specs=(HBM, HBM, VMEM, VMEM),
        scratch_shapes=[pltpu.VMEM(full.shape, BF16)] + [pltpu.VMEM(flat.shape, BF16)] * 3
        + [pltpu.VMEM((m, hid), BF16)] * 4 + [pltpu.VMEM((m, hid), F32)] * 2
        + [dma((8,)), dma((4, 3)), dma((4, 4))] + [dma((4, 8))] * 6 + [dma((1,))] * 2
        + [dma((HALO,))] * 4,
        compiler_params=params(1),
        name="gather_and_forward_halo",
    )(conv_weight, proj_weight, flat, cot)


ORDER = (2, 1, 3, 0)
PASSES = ((1, 3), (0, 2))
NT = (((1,), (1,)), ((), ()))
TN = (((0,), (0,)), ((), ()))


def backward_kernel(scale, hg_ref, acted_hbm, cot_hbm, gated_hbm, x_hbm, w_hbm,
                    grads_ref, outputs_hbm, input_grad_hbm,
                    acted_ref, cot_ref, gated_ref, x_buf, w_buf, o_buf, g_buf, near, give, keep, got, acc,
                    x_out, x_in, z_out, z_in, load, store,
                    hzs, hzr, hxs, hxr, cs, cr, xs, xr, zs, zr, free):
    z, x, core = place()
    share = grads_ref.shape[1]
    zt = [lax.rem(z + d, 4) for d in range(4)]
    across = index(z, 1 - x, core)
    other = index(z, x, 1 - core)
    even = x == 0
    sends = jnp.logical_or(jnp.logical_and(even, z < 3), jnp.logical_and(x == 1, z > 0))
    takes = jnp.logical_or(jnp.logical_and(even, z > 0), jnp.logical_and(x == 1, z < 3))
    ahead = index(lax.rem(z + (1 - 2 * x) + 4, 4), x, core)
    w_load = pltpu.make_async_copy(w_hbm, w_buf, load.at[0])
    x_load = pltpu.make_async_copy(x_hbm, x_buf, load.at[1])
    early = [
        pltpu.make_async_copy(src, dst, load.at[2 + i])
        for i, (src, dst) in enumerate(
            ((acted_hbm, acted_ref), (cot_hbm, cot_ref), (gated_hbm, gated_ref))
        )
    ]
    for copy in early:
        copy.start()
    w_load.start()
    x_load.start()
    greet([index(zt[d], x, core) for d in (1, 2, 3)] + [across, other])
    wide = 4 * share
    tile = 256
    m, hid = hg_ref.shape
    chans = acted_ref.shape[1]
    n = m // CHUNKS

    def rows(i):
        return pl.ds(pl.multiple_of(i * n, n), n)

    half = m // HALO

    def piece(i):
        return pl.ds(i * half, half)

    def halo_x(i):
        return copy_to(hg_ref.at[piece(i), :], near.at[0, piece(i), :], hxs.at[i], hxr.at[i], across)

    def halo_z(i):
        return copy_to(near.at[0, piece(i), :], near.at[1, piece(i), :], hzs.at[i], hzr.at[i], ahead)

    def core_copy(s):
        return copy_to(give.at[s % 2], got.at[s % 2], cs.at[s], cr.at[s], other)

    def x_copy(s):
        return copy_to(x_out.at[s], x_in.at[s], xs.at[s], xr.at[s], across)

    def z_copy(s):
        j = s // 4 * 3 + s % 4
        target = index(zt[ORDER[s % 4]], x, core)
        return copy_to(z_out.at[j], z_in.at[j], zs.at[j], zr.at[j], target)

    def onward(i):
        halo_x(i).wait_recv()

        @pl.when(sends)
        def _():
            halo_z(i).start()

    def compute(s):
        if s >= 2:
            core_copy(s - 2).wait_send()
        cols = pl.ds(pl.multiple_of(zt[ORDER[s % 4]] * wide, wide), wide)
        for j, k in enumerate(PASSES[s // 4]):
            left = cot_ref if k == 3 else acted_ref

            def part(i, carry, k=k, j=j, left=left):
                t = pl.ds(pl.multiple_of(i * tile, tile), tile)
                if k == 3:
                    right = gated_ref[:, t]
                elif k == 1:
                    right = hg_ref[:, t]
                else:
                    right = near[x if k == 0 else 1 - x, :, t]
                p = lax.dot_general(left[:, cols], right, TN, preferred_element_type=F32)
                for xx in range(2):
                    lo = p[2 * xx * share:(2 * xx + 1) * share]
                    hi = p[(2 * xx + 1) * share:(2 * xx + 2) * share]
                    keep[s % 2, xx, j, :, t] = jnp.where(core == 0, lo, hi)
                    give[s % 2, xx, j, :, t] = jnp.where(core == 0, hi, lo)
                return carry

            lax.fori_loop(0, hid // tile, part, 0)
        if s >= 2:
            pl.semaphore_wait(free, 1)
        core_copy(s).start()

    def to_across(s):
        core_copy(s).wait_recv()

        def add(j, carry):
            x_out[s, j] = (keep[s % 2, 1 - x, j] + got[s % 2, 1 - x, j]).astype(BF16)
            acc[s, j] = keep[s % 2, x, j] + got[s % 2, x, j]
            return carry

        lax.fori_loop(0, 2, add, 0)
        x_copy(s).start()
        if s < 6:
            pl.semaphore_signal(free, inc=1, device_id={"seq": other}, device_id_type=MESH)

    def to_z(s):
        x_copy(s).wait_recv()
        for j in range(2):
            z_out[s // 4 * 3 + s % 4, j] = (acc[s, j] + x_in[s, j].astype(F32)).astype(BF16)
        z_copy(s).start()

    span = 512

    def out_store(i):
        return pltpu.make_async_copy(o_buf.at[rows(i), :], outputs_hbm.at[rows(i), :], store.at[i])

    def grad_store(i):
        return pltpu.make_async_copy(
            g_buf.at[rows(i), :], input_grad_hbm.at[rows(i), :], store.at[CHUNKS + i]
        )

    def project(i, carry):
        def part(j, c):
            t = pl.ds(pl.multiple_of(j * span, span), span)
            p = lax.dot_general(gated_ref[rows(i), :], w_buf[3, t, :], NT, preferred_element_type=F32)
            o_buf[rows(i), t] = (x_buf[rows(i), t].astype(F32) + p).astype(BF16)
            return c

        lax.fori_loop(0, chans // span, part, 0)
        out_store(i).start()
        return carry

    def spread(i, carry):
        def part(j, c):
            t = pl.ds(pl.multiple_of(j * span, span), span)
            p = lax.dot_general(hg_ref[rows(i), :], w_buf[2, t, :], NT, preferred_element_type=F32)
            p += lax.dot_general(near[x, rows(i), :], w_buf[0, t, :], NT, preferred_element_type=F32)
            p += lax.dot_general(near[1 - x, rows(i), :], w_buf[1, t, :], NT, preferred_element_type=F32)
            slope = gelu_parts(x_buf[rows(i), t].astype(F32))[1]
            g_buf[rows(i), t] = (cot_ref[rows(i), t].astype(F32) + p * slope).astype(BF16)
            return c

        lax.fori_loop(0, chans // span, part, 0)
        grad_store(i).start()
        return carry

    for i in range(HALO):
        halo_x(i).start()

    @pl.when(jnp.logical_not(takes))
    def _():
        near[1] = jnp.zeros((m, hid), BF16)

    for copy in early:
        copy.wait()
    compute(0)
    compute(1)
    onward(0)
    onward(1)
    onward(2)
    onward(3)
    w_load.wait()
    x_load.wait()
    lax.fori_loop(0, 2, project, 0)
    onward(4)
    onward(5)
    to_across(0)
    compute(2)
    onward(6)
    onward(7)
    to_across(1)
    compute(3)
    to_across(2)
    to_across(3)
    lax.fori_loop(2, CHUNKS, project, 0)
    to_z(0)

    @pl.when(takes)
    def _():
        for i in range(HALO):
            halo_z(i).wait_recv()

    compute(4)
    to_z(1)
    compute(5)
    to_across(4)
    to_z(2)
    compute(6)
    to_across(5)
    compute(7)
    to_across(6)
    to_across(7)
    to_z(4)
    lax.fori_loop(0, 2, spread, 0)
    to_z(5)
    lax.fori_loop(2, CHUNKS, spread, 0)
    to_z(6)
    for s in (3, 7):
        x_copy(s).wait_recv()
        for j in range(s // 4 * 3, s // 4 * 3 + 3):
            z_copy(s // 4 * 4 + j % 3).wait_recv()
        for j in range(2):
            own = acc[s, j] + x_in[s, j].astype(F32)
            for i in range(s // 4 * 3, s // 4 * 3 + 3):
                own = own + z_in[i, j].astype(F32)
            grads_ref[PASSES[s // 4][j]] = own * scale
    for i in range(CHUNKS):
        out_store(i).wait()
        grad_store(i).wait()
    for i in range(HALO):
        halo_x(i).wait_send()

    @pl.when(sends)
    def _():
        for i in range(HALO):
            halo_z(i).wait_send()

    core_copy(6).wait_send()
    core_copy(7).wait_send()
    for s in range(8):
        x_copy(s).wait_send()
        if s % 4 < 3:
            z_copy(s).wait_send()


def backward(scale, hg, acted, cot, gated, rows, full):
    m, hid = hg.shape
    chans = acted.shape[1]
    share = chans // SEQ
    dma = pltpu.SemaphoreType.DMA
    pair = (2, 2, share, hid)
    return pl.pallas_call(
        functools.partial(backward_kernel, scale),
        out_shape=(
            jax.ShapeDtypeStruct((4, share, hid), F32),
            jax.ShapeDtypeStruct((m, chans), BF16),
            jax.ShapeDtypeStruct((m, chans), BF16),
        ),
        in_specs=[VMEM] + [HBM] * 5,
        out_specs=(VMEM, HBM, HBM),
        scratch_shapes=[
            pltpu.VMEM((m, chans), BF16),
            pltpu.VMEM((m, chans), BF16),
            pltpu.VMEM((m, hid), BF16),
            pltpu.VMEM((m, chans), BF16),
            pltpu.VMEM(full.shape, BF16),
            pltpu.VMEM((m, chans), BF16),
            pltpu.VMEM((m, chans), BF16),
            pltpu.VMEM((2, m, hid), BF16),
            pltpu.VMEM((2,) + pair, F32),
            pltpu.VMEM((2,) + pair, F32),
            pltpu.VMEM((2,) + pair, F32),
            pltpu.VMEM((8, 2, share, hid), F32),
            pltpu.VMEM((8, 2, share, hid), BF16),
            pltpu.VMEM((8, 2, share, hid), BF16),
            pltpu.VMEM((6, 2, share, hid), BF16),
            pltpu.VMEM((6, 2, share, hid), BF16),
            dma((5,)), dma((2 * CHUNKS,)),
            dma((HALO,)), dma((HALO,)), dma((HALO,)), dma((HALO,)),
            dma((8,)), dma((8,)), dma((8,)), dma((8,)), dma((6,)), dma((6,)),
            pltpu.SemaphoreType.REGULAR,
        ],
        compiler_params=params(2, 62),
        name="backward_halo_and_reduce",
    )(hg, acted, cot, gated, rows, full)


def pair_shards(inputs, conv_weight, proj_weight, cotangent):
    batch, local_len, chans = inputs.shape
    scale = 1.0 / float(batch * L) ** 0.5
    rows = inputs.reshape(-1, chans)
    cot = cotangent.reshape(-1, chans)
    full, acted, gated, hg = forward(conv_weight, proj_weight, rows, cot)
    grads, outputs, input_grad = backward(scale, hg, acted, cot, gated, rows, full)
    return (
        outputs.reshape(batch, local_len, chans),
        input_grad.reshape(batch, local_len, chans),
        grads[:3].transpose(1, 0, 2),
        grads[3],
    )


def solution(mesh):
    fast = mesh.shape["seq"] == SEQ
    return jax.shard_map(
        pair_shards if fast else shards,
        mesh=mesh,
        in_specs=(
            P("groups", "seq", None),
            P(None, "seq", None),
            P("seq", None),
            P("groups", "seq", None),
        ),
        out_specs=(
            P("groups", "seq", None),
            P("groups", "seq", None),
            P(("groups", "seq"), None, None),
            P(("groups", "seq"), None),
        ),
        check_vma=False,
    )
```

```python
import functools

import jax
import jax.numpy as jnp
from jax import lax
from jax.experimental import pallas as pl
from jax.experimental.pallas import tpu as pltpu
from jax.sharding import PartitionSpec as P

L = 8192


def from_behind(block, axis, distance):
    devices = range(lax.axis_size(axis))
    route = [(i - distance, i) for i in devices if i - distance in devices]
    return lax.ppermute(block, axis, route)


def gelu_grad(point, upstream):
    return jax.vjp(jax.nn.gelu, point)[1](upstream)[0]


def shards(inputs, conv_weight, proj_weight, cotangent):
    batch, local_len, chans = inputs.shape
    devices = lax.axis_size("seq")
    stride = devices // 8
    scale = 1.0 / float(batch * L) ** 0.5
    acted = jax.nn.gelu(inputs.astype(jnp.float32)).astype(jnp.bfloat16)
    conv_weight, proj_weight = (
        lax.all_gather(conv_weight, "seq", axis=1, tiled=True),
        lax.all_gather(proj_weight, "seq", axis=0, tiled=True),
    )
    hid = conv_weight.shape[2]
    acted_rows = acted.reshape(-1, chans)
    before = from_behind(acted, "seq", stride)
    after = from_behind(acted, "seq", -stride)
    hidden = jnp.dot(before.reshape(-1, chans), conv_weight[0], preferred_element_type=jnp.float32)
    hidden = hidden + jnp.dot(acted_rows, conv_weight[1], preferred_element_type=jnp.float32)
    hidden = hidden + jnp.dot(
        after.reshape(-1, chans), conv_weight[2], preferred_element_type=jnp.float32
    )
    gated = jax.nn.gelu(hidden).astype(jnp.bfloat16)
    outputs = (
        inputs.reshape(-1, chans).astype(jnp.float32)
        + jnp.dot(gated, proj_weight.T, preferred_element_type=jnp.float32)
    ).astype(jnp.bfloat16)
    cot_rows = cotangent.reshape(-1, chans)
    gated_grad = jnp.dot(cot_rows, proj_weight, preferred_element_type=jnp.float32)
    hidden_grad = gelu_grad(hidden, gated_grad).astype(jnp.bfloat16)
    grad_blocks = hidden_grad.reshape(batch, local_len, hid)
    grad_later = from_behind(grad_blocks, "seq", -stride).reshape(-1, hid)
    grad_earlier = from_behind(grad_blocks, "seq", stride).reshape(-1, hid)
    acted_grad = jnp.dot(grad_later, conv_weight[0].T, preferred_element_type=jnp.float32)
    acted_grad = acted_grad + jnp.dot(
        hidden_grad, conv_weight[1].T, preferred_element_type=jnp.float32
    )
    acted_grad = acted_grad + jnp.dot(
        grad_earlier, conv_weight[2].T, preferred_element_type=jnp.float32
    )
    input_grad = (
        cot_rows.astype(jnp.float32)
        + gelu_grad(inputs.reshape(-1, chans).astype(jnp.float32), acted_grad)
    ).astype(jnp.bfloat16)
    tap_grads = (grad_later, hidden_grad, grad_earlier)
    share = chans // devices
    local_terms = [
        jnp.dot(acted_rows.T, piece, preferred_element_type=jnp.float32) for piece in tap_grads
    ]
    local_terms.append(jnp.dot(cot_rows.T, gated, preferred_element_type=jnp.float32))
    stacked = jnp.stack(local_terms, axis=1)
    received = lax.all_to_all(stacked, "seq", split_axis=0, concat_axis=0, tiled=True)
    summed = jnp.sum(received.reshape(devices, share, 4, received.shape[2]), axis=0)
    conv_sum = summed[:, 0:3, :]
    proj_sum = summed[:, 3, :]
    return (
        outputs.reshape(batch, local_len, chans),
        input_grad.reshape(batch, local_len, chans),
        conv_sum * scale,
        proj_sum * scale,
    )


F32 = jnp.float32
BF16 = jnp.bfloat16
MESH = pl.DeviceIdType.MESH
VMEM = pl.BlockSpec(memory_space=pltpu.VMEM)
HBM = pl.BlockSpec(memory_space=pl.ANY)
SEQ = 16
CHUNKS = 4
HALO = 8
COEF = 0.7978845608028654
CUBE = 0.044715


def place():
    s = lax.axis_index("seq")
    return s // 4, (s // 2) % 2, s % 2


def index(z, x, core):
    return (z * 2 + x) * 2 + core


def copy_to(src, dst, send, recv, target):
    return pltpu.make_async_remote_copy(
        src_ref=src, dst_ref=dst, send_sem=send, recv_sem=recv,
        device_id={"seq": target}, device_id_type=MESH,
    )


def gelu_parts(v):
    t = jnp.tanh(COEF * (v + CUBE * v * v * v))
    half = 0.5 * (1.0 + t)
    return half * v, half + (0.5 * COEF) * v * (1.0 - t * t) * (1.0 + (3.0 * CUBE) * v * v)


def params(cid, mib=56):
    return pltpu.CompilerParams(
        collective_id=cid, has_side_effects=True, vmem_limit_bytes=mib * 1024 * 1024
    )


ORDER = (2, 1, 3, 0)
PASSES = ((1, 3), (0, 2))
NT = (((1,), (1,)), ((), ()))
TN = (((0,), (0,)), ((), ()))


def block_kernel(scale, conv_hbm, proj_hbm, x_hbm, cot_hbm, grads_ref, outputs_hbm, input_grad_hbm,
                 w_buf, x_ref, cot_ref, acted_ref, out_a, in_a, out_s, in_s, part, gg, gated_ref, hg_ref,
                 o_buf, near, give, keep, got, acc, x_out, x_in, z_out, z_in, own_sem, store,
                 zs, zr, xs, xr, ys, yr, cs, cr, os, orv, hzs, hzr, hxs, hxr,
                 bzs, bzr, bxs, bxr, rcs, rcr, rxs, rxr, rzs, rzr, free):
    z, x, core = place()
    group = lax.axis_index("groups")
    me = lax.axis_index("seq")
    share = proj_hbm.shape[0]
    across = index(z, 1 - x, core)
    other = index(z, x, 1 - core)
    origin = (z + 1 - 2 * lax.rem(z, 2), 2 - z // 2, 3 - 3 * (z // 2), z)
    up = x == 1
    sends = jnp.logical_or(jnp.logical_and(up, z < 3), jnp.logical_and(x == 0, z > 0))
    takes = jnp.logical_or(jnp.logical_and(up, z > 0), jnp.logical_and(x == 0, z < 3))
    ahead = index(lax.rem(z + (2 * x - 1) + 4, 4), x, core)

    mine = pl.ds(pl.multiple_of(me * share, share), share)
    loads = [
        pltpu.make_async_copy(conv_hbm.at[tap], w_buf.at[slot, mine, :], own_sem.at[slot])
        for slot, tap in enumerate((0, 2, 1))
    ]
    loads.append(pltpu.make_async_copy(proj_hbm, w_buf.at[3, mine, :], own_sem.at[3]))
    x_load = pltpu.make_async_copy(x_hbm, x_ref, own_sem.at[4])
    cot_load = pltpu.make_async_copy(cot_hbm, cot_ref, own_sem.at[5])
    for load in loads:
        load.start()
    x_load.start()
    cot_load.start()
    barrier = pltpu.get_barrier_semaphore()
    for target in [index(origin[j], x, core) for j in range(3)] + [across, other]:
        pl.semaphore_signal(barrier, inc=1, device_id={"seq": target}, device_id_type=MESH)
    pl.semaphore_signal(
        barrier, inc=1, device_id={"groups": 1 - group, "seq": me}, device_id_type=MESH
    )
    pl.semaphore_wait(barrier, 6)

    slots = (1 - x, x, 2, 3)
    half = share // 2

    def piece(p, j, xx, start, size):
        begin = pl.multiple_of(index(origin[j], xx, core) * share + start, 16)
        return w_buf.at[slots[p], pl.ds(begin, size), :]

    def plane(p, j, xx):
        return piece(p, j, xx, group * half, half)

    def z_copy(q, d):
        place_ = plane((0, 0, 2, 3)[q], 3, 1 - x if q == 1 else x)
        return copy_to(place_, place_, zs.at[q, d], zr.at[q, z], index(origin[d], x, core))

    def z_came(q, j):
        place_ = plane((0, 0, 2, 3)[q], j, 1 - x if q == 1 else x)
        copy_to(place_, place_, zs.at[q, 0], zr.at[q, origin[j]], across).wait_recv()

    def z_begin(q):
        for d in range(3):
            z_copy(q, d).start()

    def x_copy(p, j):
        place_ = plane(1 - p if p < 2 else p, j % 4, x if j < 4 else 1 - x)
        return copy_to(place_, place_, xs.at[p, j], xr.at[p, j], across)

    def x_came(p, j):
        place_ = plane(p, j % 4, 1 - x if j < 4 else x)
        copy_to(place_, place_, xs.at[p, j], xr.at[p, j], across).wait_recv()

    def column(j):
        return j % 4, (x if j < 4 else 1 - x)

    def y_copy(p, j, whose):
        place_ = piece(p, *column(j), whose * half, half)
        return pltpu.make_async_remote_copy(
            src_ref=place_, dst_ref=place_, send_sem=ys.at[p, j], recv_sem=yr.at[p, j],
            device_id={"groups": 1 - group, "seq": me}, device_id_type=MESH,
        )

    def core_copy(p, j):
        place_ = piece(p, *column(j), 0, share)
        return copy_to(place_, place_, cs.at[p, j], cr.at[p, j], other)

    def own_core():
        place_ = w_buf.at[:, mine, :]
        return copy_to(place_, place_, os.at[0], orv.at[0], other)

    def own_core_came():
        start = pl.multiple_of(other * share, 16)
        place_ = w_buf.at[:, pl.ds(start, share), :]
        copy_to(place_, place_, os.at[0], orv.at[0], other).wait_recv()

    def take_z(q, j):
        z_came(q, j)
        p = (0, 0, 2, 3)[q]
        y_copy(p, j + 4 if q == 1 else j, group).start()
        x_copy(1 if q < 2 else q, j + 4 if q == 1 else j).start()

    def take_z_early(q, j):
        z_came(q, j)
        x_copy(q, j).start()

    def take_x(p, j):
        x_came(p, j)
        y_copy(p, j + 4 if j < 4 else j - 4, group).start()

    def take_y(p, j):
        y_copy(p, j, 1 - group).wait_recv()
        core_copy(p, j).start()

    def core_came(p):
        for j in swapped:
            place_ = w_buf.at[
                slots[p],
                pl.ds(pl.multiple_of(index(origin[j % 4], x if j < 4 else 1 - x, 1 - core) * share, 16), share),
                :,
            ]
            copy_to(place_, place_, cs.at[p, j], cr.at[p, j], other).wait_recv()

    swapped = (0, 1, 2, 4, 5, 6, 7)
    x_sent = ((0, 3),) + tuple((1, j) for j in range(7)) + tuple((p, j) for p in (2, 3) for j in range(4))
    m = acted_ref.shape[0]
    n = m // CHUNKS
    h = m // HALO

    def rows(i):
        return pl.ds(pl.multiple_of(i * n, n), n)

    def part_rows(i):
        return pl.ds(pl.multiple_of(i * h, h), h)

    def halo_z(i):
        r = part_rows(i)
        return copy_to(out_a.at[r, :], in_a.at[r, :], hzs.at[i], hzr.at[i], ahead)

    def halo_x(i):
        r = part_rows(i)
        return copy_to(out_s.at[r, :], in_s.at[r, :], hxs.at[i], hxr.at[i], across)

    tile = 64

    def act(i, carry):
        r = pl.ds(pl.multiple_of(i * tile, tile), tile)
        v = x_ref[r, :].astype(F32)
        t = jnp.tanh(COEF * (v + CUBE * v * v * v))
        acted_ref[r, :] = (0.5 * v * (1.0 + t)).astype(BF16)
        return carry

    def far_part(i, carry):
        out_a[rows(i), :] = jnp.dot(
            acted_ref[rows(i), :], w_buf[1 - x], preferred_element_type=F32
        ).astype(BF16)

        @pl.when(sends)
        def _():
            for k in range(HALO // CHUNKS):
                halo_z(i * (HALO // CHUNKS) + k).start()
        return carry

    def near_part(i, carry):
        part[rows(i), :] = jnp.dot(acted_ref[rows(i), :], w_buf[x], preferred_element_type=F32)
        return carry

    def combine(i):
        r = part_rows(i)

        @pl.when(takes)
        def _():
            halo_z(i).wait_recv()
            part[r, :] = part[r, :] + in_a[r, :].astype(F32)
        out_s[r, :] = part[r, :].astype(BF16)
        halo_x(i).start()

    def middle(i):
        part[rows(i), :] = jnp.dot(acted_ref[rows(i), :], w_buf[2], preferred_element_type=F32)
        gg[rows(i), :] = jnp.dot(cot_ref[rows(i), :], w_buf[3], preferred_element_type=F32)

    def finish(i):
        r = part_rows(i)
        halo_x(i).wait_recv()
        hidden = part[r, :] + in_s[r, :].astype(F32)
        value, slope = gelu_parts(hidden)
        gated_ref[r, :] = value.astype(BF16)
        hg_ref[r, :] = (gg[r, :] * slope).astype(BF16)
        back_x(i).start()

    wide = 4 * share
    wide_tile = 256
    hid = hg_ref.shape[1]
    chans = acted_ref.shape[1]
    even = x == 0
    back_sends = jnp.logical_or(jnp.logical_and(even, z < 3), jnp.logical_and(x == 1, z > 0))
    back_takes = jnp.logical_or(jnp.logical_and(even, z > 0), jnp.logical_and(x == 1, z < 3))
    back_ahead = index(lax.rem(z + (1 - 2 * x) + 4, 4), x, core)
    zt = [lax.rem(z + d, 4) for d in range(4)]

    def back_x(i):
        r = part_rows(i)
        return copy_to(hg_ref.at[r, :], near.at[0, r, :], bxs.at[i], bxr.at[i], across)

    def back_z(i):
        r = part_rows(i)
        return copy_to(near.at[0, r, :], near.at[1, r, :], bzs.at[i], bzr.at[i], back_ahead)

    def sum_core(s):
        return copy_to(give.at[s % 2], got.at[s % 2], rcs.at[s], rcr.at[s], other)

    def sum_x(s):
        return copy_to(x_out.at[s], x_in.at[s], rxs.at[s], rxr.at[s], across)

    def sum_z(s):
        j = s // 4 * 3 + s % 4
        target = index(zt[ORDER[s % 4]], x, core)
        return copy_to(z_out.at[j], z_in.at[j], rzs.at[j], rzr.at[j], target)

    def onward(i):
        back_x(i).wait_recv()

        @pl.when(back_sends)
        def _():
            back_z(i).start()

    def compute(s):
        if s >= 2:
            sum_core(s - 2).wait_send()
        cols = pl.ds(pl.multiple_of(zt[ORDER[s % 4]] * wide, wide), wide)
        for j, k in enumerate(PASSES[s // 4]):
            left = cot_ref if k == 3 else acted_ref

            def term(i, carry, k=k, j=j, left=left):
                t = pl.ds(pl.multiple_of(i * wide_tile, wide_tile), wide_tile)
                if k == 3:
                    right = gated_ref[:, t]
                elif k == 1:
                    right = hg_ref[:, t]
                else:
                    right = near[x if k == 0 else 1 - x, :, t]
                p = lax.dot_general(left[:, cols], right, TN, preferred_element_type=F32)
                for xx in range(2):
                    lo = p[2 * xx * share:(2 * xx + 1) * share]
                    hi = p[(2 * xx + 1) * share:(2 * xx + 2) * share]
                    keep[s % 2, xx, j, :, t] = jnp.where(core == 0, lo, hi)
                    give[s % 2, xx, j, :, t] = jnp.where(core == 0, hi, lo)
                return carry

            lax.fori_loop(0, hid // wide_tile, term, 0)
        if s >= 2:
            pl.semaphore_wait(free, 1)
        sum_core(s).start()

    def to_across(s):
        sum_core(s).wait_recv()

        def add(j, carry):
            x_out[s, j] = (keep[s % 2, 1 - x, j] + got[s % 2, 1 - x, j]).astype(BF16)
            acc[s, j] = keep[s % 2, x, j] + got[s % 2, x, j]
            return carry

        lax.fori_loop(0, 2, add, 0)
        sum_x(s).start()
        if s < 6:
            pl.semaphore_signal(free, inc=1, device_id={"seq": other}, device_id_type=MESH)

    def to_z(s):
        sum_x(s).wait_recv()
        for j in range(2):
            z_out[s // 4 * 3 + s % 4, j] = (acc[s, j] + x_in[s, j].astype(F32)).astype(BF16)
        sum_z(s).start()

    span = 512

    def out_store(i):
        return pltpu.make_async_copy(o_buf.at[rows(i), :], outputs_hbm.at[rows(i), :], store.at[i])

    def grad_store(i):
        return pltpu.make_async_copy(
            cot_ref.at[rows(i), :], input_grad_hbm.at[rows(i), :], store.at[CHUNKS + i]
        )

    def project(i, carry):
        def span_part(j, c):
            t = pl.ds(pl.multiple_of(j * span, span), span)
            p = lax.dot_general(gated_ref[rows(i), :], w_buf[3, t, :], NT, preferred_element_type=F32)
            o_buf[rows(i), t] = (x_ref[rows(i), t].astype(F32) + p).astype(BF16)
            return c

        lax.fori_loop(0, chans // span, span_part, 0)
        out_store(i).start()
        return carry

    def spread(i, carry):
        def span_part(j, c):
            t = pl.ds(pl.multiple_of(j * span, span), span)
            p = lax.dot_general(hg_ref[rows(i), :], w_buf[2, t, :], NT, preferred_element_type=F32)
            p += lax.dot_general(near[x, rows(i), :], w_buf[0, t, :], NT, preferred_element_type=F32)
            p += lax.dot_general(near[1 - x, rows(i), :], w_buf[1, t, :], NT, preferred_element_type=F32)
            slope = gelu_parts(x_ref[rows(i), t].astype(F32))[1]
            cot_ref[rows(i), t] = (cot_ref[rows(i), t].astype(F32) + p * slope).astype(BF16)
            return c

        lax.fori_loop(0, chans // span, span_part, 0)
        grad_store(i).start()
        return carry

    for load in loads:
        load.wait()
    z_begin(0)
    x_copy(0, 3).start()
    own_core().start()
    x_copy(1, 3).start()
    x_load.wait()
    steps = m // tile
    lax.fori_loop(0, steps // 2, act, 0)
    take_x(0, 3)
    z_begin(1)
    lax.fori_loop(steps // 2, steps, act, 0)
    take_z(0, 0)
    take_z(0, 1)
    take_x(1, 3)
    take_z(0, 2)
    z_begin(2)
    z_begin(3)
    take_y(0, 7)
    take_x(1, 0)
    take_z(1, 0)
    take_y(0, 0)
    take_x(1, 1)
    take_z(1, 1)
    take_y(0, 1)
    take_x(1, 2)
    take_y(0, 2)
    take_z(1, 2)
    x_copy(2, 3).start()
    x_copy(3, 3).start()
    take_z_early(2, 0)
    take_y(0, 4)
    take_x(1, 4)
    take_y(0, 5)
    take_x(1, 5)
    take_z_early(2, 1)
    take_y(0, 6)
    own_core_came()
    core_came(0)
    lax.fori_loop(0, 2, far_part, 0)
    take_x(1, 6)
    y_copy(2, 0, group).start()
    y_copy(2, 1, group).start()
    lax.fori_loop(2, CHUNKS, far_part, 0)
    take_z(2, 2)
    take_x(2, 3)
    take_x(3, 3)
    take_y(1, 7)
    take_z(3, 0)
    take_y(1, 4)
    take_y(1, 5)
    take_x(2, 0)
    take_z(3, 1)
    take_y(1, 6)
    take_x(2, 1)
    take_y(1, 0)
    take_y(1, 1)
    take_z(3, 2)
    take_x(2, 2)
    take_y(1, 2)
    core_came(1)
    lax.fori_loop(0, CHUNKS, near_part, 0)
    take_x(3, 0)
    combine(0)
    take_x(3, 1)
    take_x(3, 2)
    for j in (0, 1, 2, 7):
        take_y(2, j)
    combine(1)
    for j in (4, 5, 6):
        take_y(2, j)
    combine(2)
    for j in (7, 0, 1, 4):
        take_y(3, j)
    combine(3)
    for j in (2, 5, 6):
        take_y(3, j)
    cot_load.wait()
    combine(4)
    core_came(2)
    core_came(3)
    middle(0)
    combine(5)
    middle(1)
    combine(6)
    middle(2)
    combine(7)
    middle(3)
    for i in range(HALO):
        finish(i)

    @pl.when(jnp.logical_not(back_takes))
    def _():
        near[1] = jnp.zeros((m, hid), BF16)

    project(0, 0)
    compute(0)
    onward(0)
    project(1, 0)
    onward(1)
    compute(1)
    to_across(0)
    onward(2)
    compute(2)
    onward(3)
    to_across(1)
    compute(3)
    onward(4)
    to_across(2)
    project(2, 0)
    project(3, 0)
    onward(5)
    to_across(3)
    onward(6)
    onward(7)
    to_z(0)

    @pl.when(back_takes)
    def _():
        for i in range(HALO):
            back_z(i).wait_recv()

    compute(4)
    to_z(1)
    compute(5)
    to_across(4)
    to_z(2)
    compute(6)
    to_across(5)
    compute(7)
    to_across(6)
    to_across(7)
    lax.fori_loop(0, 2, spread, 0)
    to_z(4)
    lax.fori_loop(2, CHUNKS, spread, 0)
    to_z(5)
    to_z(6)
    for s in (3, 7):
        sum_x(s).wait_recv()
        for j in range(s // 4 * 3, s // 4 * 3 + 3):
            sum_z(s // 4 * 4 + j % 3).wait_recv()
        for j in range(2):
            own = acc[s, j] + x_in[s, j].astype(F32)
            for i in range(s // 4 * 3, s // 4 * 3 + 3):
                own = own + z_in[i, j].astype(F32)
            grads_ref[PASSES[s // 4][j]] = own * scale
    for i in range(CHUNKS):
        out_store(i).wait()
        grad_store(i).wait()
    own_core().wait_send()
    for q in range(4):
        for d in range(3):
            z_copy(q, d).wait_send()
    for p, j in x_sent:
        x_copy(p, j).wait_send()
    for p in range(4):
        for j in swapped:
            y_copy(p, j, group).wait_send()
            core_copy(p, j).wait_send()
    for i in range(HALO):
        halo_x(i).wait_send()
        back_x(i).wait_send()

    @pl.when(sends)
    def _():
        for i in range(HALO):
            halo_z(i).wait_send()

    @pl.when(back_sends)
    def _():
        for i in range(HALO):
            back_z(i).wait_send()

    sum_core(6).wait_send()
    sum_core(7).wait_send()
    for s in range(8):
        sum_x(s).wait_send()
        if s % 4 < 3:
            sum_z(s).wait_send()


def block(scale, conv_weight, proj_weight, flat, cot):
    share, hid = proj_weight.shape
    m, chans = flat.shape
    dma = pltpu.SemaphoreType.DMA
    pair = (2, 2, share, hid)
    halo = pltpu.VMEM((m, hid), BF16)
    wide = pltpu.VMEM((m, chans), BF16)
    return pl.pallas_call(
        functools.partial(block_kernel, scale),
        out_shape=(
            jax.ShapeDtypeStruct((4, share, hid), F32),
            jax.ShapeDtypeStruct((m, chans), BF16),
            jax.ShapeDtypeStruct((m, chans), BF16),
        ),
        in_specs=[HBM] * 4,
        out_specs=(VMEM, HBM, HBM),
        scratch_shapes=[pltpu.VMEM((4, chans, hid), BF16), wide, wide, wide]
        + [halo] * 4 + [pltpu.VMEM((m, hid), F32)] * 2 + [halo] * 2
        + [wide, pltpu.VMEM((2, m, hid), BF16)]
        + [pltpu.VMEM((2,) + pair, F32)] * 3
        + [pltpu.VMEM((8, 2, share, hid), F32)]
        + [pltpu.VMEM((8, 2, share, hid), BF16)] * 2
        + [pltpu.VMEM((6, 2, share, hid), BF16)] * 2
        + [dma((8,)), dma((2 * CHUNKS,)), dma((4, 3)), dma((4, 4))] + [dma((4, 8))] * 6
        + [dma((1,))] * 2 + [dma((HALO,))] * 8 + [dma((8,))] * 4 + [dma((6,))] * 2
        + [pltpu.SemaphoreType.REGULAR],
        compiler_params=params(1, 62),
        name="block_step",
    )(conv_weight, proj_weight, flat, cot)


def deliver_kernel(grads, outputs_in, input_grad_in, outputs, input_grad, conv, proj,
                   held_grads, held_out, held_in, came, gone):
    parts = 4
    m = outputs_in.shape[0] // parts
    moves = []
    for i in range(parts):
        r = pl.ds(i * m, m)
        moves.append((outputs_in.at[r, :], held_out.at[r, :], outputs.at[r, :]))
        moves.append((input_grad_in.at[r, :], held_in.at[r, :], input_grad.at[r, :]))
    moves.append((grads.at[pl.ds(0, 3)], held_grads.at[pl.ds(0, 3)], conv))
    moves.append((grads.at[3], held_grads.at[3], proj))
    loads = [pltpu.make_async_copy(s, h, came.at[i]) for i, (s, h, _) in enumerate(moves)]
    stores = [pltpu.make_async_copy(h, d, gone.at[i]) for i, (_, h, d) in enumerate(moves)]
    for load in loads:
        load.start()
    for load, store in zip(loads, stores):
        load.wait()
        store.start()
    for store in stores:
        store.wait()


def deliver(grads, outputs, input_grad):
    like = lambda shape, kind: jax.ShapeDtypeStruct(shape, kind)
    return pl.pallas_call(
        deliver_kernel,
        out_shape=(
            like(outputs.shape, BF16), like(input_grad.shape, BF16),
            like((3,) + grads.shape[1:], F32), like(grads.shape[1:], F32),
        ),
        in_specs=[pl.BlockSpec(memory_space=pltpu.HBM)] * 3,
        out_specs=(HBM,) * 4,
        scratch_shapes=[pltpu.VMEM(grads.shape, F32), pltpu.VMEM(outputs.shape, BF16),
                        pltpu.VMEM(outputs.shape, BF16)]
        + [pltpu.SemaphoreType.DMA((10,))] * 2,
        compiler_params=pltpu.CompilerParams(vmem_limit_bytes=62 * 1024 * 1024),
        name="deliver",
    )(grads, outputs, input_grad)


def pair_shards(inputs, conv_weight, proj_weight, cotangent):
    batch, local_len, chans = inputs.shape
    scale = 1.0 / float(batch * L) ** 0.5
    rows = inputs.reshape(-1, chans)
    cot = cotangent.reshape(-1, chans)
    outputs, input_grad, conv, proj = deliver(*block(scale, conv_weight, proj_weight, rows, cot))
    return (
        outputs.reshape(batch, local_len, chans),
        input_grad.reshape(batch, local_len, chans),
        conv.transpose(1, 0, 2),
        proj,
    )


def solution(mesh):
    fast = mesh.shape["seq"] == SEQ
    return jax.shard_map(
        pair_shards if fast else shards,
        mesh=mesh,
        in_specs=(
            P("groups", "seq", None),
            P(None, "seq", None),
            P("seq", None),
            P("groups", "seq", None),
        ),
        out_specs=(
            P("groups", "seq", None),
            P("groups", "seq", None),
            P(("groups", "seq"), None, None),
            P(("groups", "seq"), None),
        ),
        check_vma=False,
    )
```

```python
import functools

import jax
import jax.numpy as jnp
from jax import lax
from jax.experimental import pallas as pl
from jax.experimental.pallas import tpu as pltpu
from jax.sharding import PartitionSpec as P

L = 8192


def from_behind(block, axis, distance):
    devices = range(lax.axis_size(axis))
    route = [(i - distance, i) for i in devices if i - distance in devices]
    return lax.ppermute(block, axis, route)


def gelu_grad(point, upstream):
    return jax.vjp(jax.nn.gelu, point)[1](upstream)[0]


def shards(inputs, conv_weight, proj_weight, cotangent):
    batch, local_len, chans = inputs.shape
    devices = lax.axis_size("seq")
    stride = devices // 8
    scale = 1.0 / float(batch * L) ** 0.5
    acted = jax.nn.gelu(inputs.astype(jnp.float32)).astype(jnp.bfloat16)
    conv_weight, proj_weight = (
        lax.all_gather(conv_weight, "seq", axis=1, tiled=True),
        lax.all_gather(proj_weight, "seq", axis=0, tiled=True),
    )
    hid = conv_weight.shape[2]
    acted_rows = acted.reshape(-1, chans)
    before = from_behind(acted, "seq", stride)
    after = from_behind(acted, "seq", -stride)
    hidden = jnp.dot(before.reshape(-1, chans), conv_weight[0], preferred_element_type=jnp.float32)
    hidden = hidden + jnp.dot(acted_rows, conv_weight[1], preferred_element_type=jnp.float32)
    hidden = hidden + jnp.dot(
        after.reshape(-1, chans), conv_weight[2], preferred_element_type=jnp.float32
    )
    gated = jax.nn.gelu(hidden).astype(jnp.bfloat16)
    outputs = (
        inputs.reshape(-1, chans).astype(jnp.float32)
        + jnp.dot(gated, proj_weight.T, preferred_element_type=jnp.float32)
    ).astype(jnp.bfloat16)
    cot_rows = cotangent.reshape(-1, chans)
    gated_grad = jnp.dot(cot_rows, proj_weight, preferred_element_type=jnp.float32)
    hidden_grad = gelu_grad(hidden, gated_grad).astype(jnp.bfloat16)
    grad_blocks = hidden_grad.reshape(batch, local_len, hid)
    grad_later = from_behind(grad_blocks, "seq", -stride).reshape(-1, hid)
    grad_earlier = from_behind(grad_blocks, "seq", stride).reshape(-1, hid)
    acted_grad = jnp.dot(grad_later, conv_weight[0].T, preferred_element_type=jnp.float32)
    acted_grad = acted_grad + jnp.dot(
        hidden_grad, conv_weight[1].T, preferred_element_type=jnp.float32
    )
    acted_grad = acted_grad + jnp.dot(
        grad_earlier, conv_weight[2].T, preferred_element_type=jnp.float32
    )
    input_grad = (
        cot_rows.astype(jnp.float32)
        + gelu_grad(inputs.reshape(-1, chans).astype(jnp.float32), acted_grad)
    ).astype(jnp.bfloat16)
    tap_grads = (grad_later, hidden_grad, grad_earlier)
    share = chans // devices
    local_terms = [
        jnp.dot(acted_rows.T, piece, preferred_element_type=jnp.float32) for piece in tap_grads
    ]
    local_terms.append(jnp.dot(cot_rows.T, gated, preferred_element_type=jnp.float32))
    stacked = jnp.stack(local_terms, axis=1)
    received = lax.all_to_all(stacked, "seq", split_axis=0, concat_axis=0, tiled=True)
    summed = jnp.sum(received.reshape(devices, share, 4, received.shape[2]), axis=0)
    conv_sum = summed[:, 0:3, :]
    proj_sum = summed[:, 3, :]
    return (
        outputs.reshape(batch, local_len, chans),
        input_grad.reshape(batch, local_len, chans),
        conv_sum * scale,
        proj_sum * scale,
    )


F32 = jnp.float32
BF16 = jnp.bfloat16
MESH = pl.DeviceIdType.MESH
VMEM = pl.BlockSpec(memory_space=pltpu.VMEM)
HBM = pl.BlockSpec(memory_space=pl.ANY)
SEQ = 16
CHUNKS = 4
HALO = 8
COEF = 0.7978845608028654
CUBE = 0.044715


def place():
    s = lax.axis_index("seq")
    return s // 4, (s // 2) % 2, s % 2


def index(z, x, core):
    return (z * 2 + x) * 2 + core


def copy_to(src, dst, send, recv, target):
    return pltpu.make_async_remote_copy(
        src_ref=src, dst_ref=dst, send_sem=send, recv_sem=recv,
        device_id={"seq": target}, device_id_type=MESH,
    )


def gelu_parts(v):
    t = jnp.tanh(COEF * (v + CUBE * v * v * v))
    half = 0.5 * (1.0 + t)
    return half * v, half + (0.5 * COEF) * v * (1.0 - t * t) * (1.0 + (3.0 * CUBE) * v * v)


def params(cid, mib=56):
    return pltpu.CompilerParams(
        collective_id=cid, has_side_effects=True, vmem_limit_bytes=mib * 1024 * 1024
    )


PASSES = ((1, 3), (0, 2))
NT = (((1,), (1,)), ((), ()))
TN = (((0,), (0,)), ((), ()))


def block_kernel(scale, conv_hbm, proj_hbm, x_hbm, cot_hbm, grads_ref, o_buf, g_buf,
                 w_buf, x_ref, cot_ref, acted_ref, out_a, in_a, out_s, in_s, sums, gated_ref, hg_ref,
                 near, give, keep, got, x_out, x_in, z_out, z_in, own_sem,
                 zs, zr, xs, xr, ys, yr, cs, cr, os, orv, hzs, hzr, hxs, hxr,
                 bzs, bzr, bxs, bxr, rcs, rcr, rxs, rxr, rzs, rzr, free):
    z, x, core = place()
    group = lax.axis_index("groups")
    me = lax.axis_index("seq")
    share = proj_hbm.shape[0]
    across = index(z, 1 - x, core)
    other = index(z, x, 1 - core)
    origin = (z + 1 - 2 * lax.rem(z, 2), 2 - z // 2, 3 - 3 * (z // 2), z)
    up = x == 1
    sends = jnp.logical_or(jnp.logical_and(up, z < 3), jnp.logical_and(x == 0, z > 0))
    takes = jnp.logical_or(jnp.logical_and(up, z > 0), jnp.logical_and(x == 0, z < 3))
    ahead = index(lax.rem(z + (2 * x - 1) + 4, 4), x, core)

    mine = pl.ds(pl.multiple_of(me * share, share), share)
    loads = [
        pltpu.make_async_copy(conv_hbm.at[tap], w_buf.at[slot, mine, :], own_sem.at[slot])
        for slot, tap in enumerate((0, 2, 1))
    ]
    loads.append(pltpu.make_async_copy(proj_hbm, w_buf.at[3, mine, :], own_sem.at[3]))
    x_load = pltpu.make_async_copy(x_hbm, x_ref, own_sem.at[4])
    cot_load = pltpu.make_async_copy(cot_hbm, cot_ref, own_sem.at[5])
    for load in loads:
        load.start()
    x_load.start()
    cot_load.start()
    barrier = pltpu.get_barrier_semaphore()
    for target in [index(origin[j], x, core) for j in range(3)] + [across, other]:
        pl.semaphore_signal(barrier, inc=1, device_id={"seq": target}, device_id_type=MESH)
    pl.semaphore_signal(
        barrier, inc=1, device_id={"groups": 1 - group, "seq": me}, device_id_type=MESH
    )
    pl.semaphore_wait(barrier, 6)

    slots = (1 - x, x, 2, 3)
    part = sums.at[pl.ds(0, acted_ref.shape[0]), :]
    gg = sums.at[pl.ds(acted_ref.shape[0], acted_ref.shape[0]), :]
    half = share // 2

    def piece(p, j, xx, start, size):
        begin = pl.multiple_of(index(origin[j], xx, core) * share + start, 16)
        return w_buf.at[slots[p], pl.ds(begin, size), :]

    def plane(p, j, xx):
        return piece(p, j, xx, group * half, half)

    def z_copy(q, d):
        place_ = plane((0, 0, 2, 3)[q], 3, 1 - x if q == 1 else x)
        return copy_to(place_, place_, zs.at[q, d], zr.at[q, z], index(origin[d], x, core))

    def z_came(q, j):
        place_ = plane((0, 0, 2, 3)[q], j, 1 - x if q == 1 else x)
        copy_to(place_, place_, zs.at[q, 0], zr.at[q, origin[j]], across).wait_recv()

    def z_begin(q):
        for d in range(3):
            z_copy(q, d).start()

    def x_copy(p, j):
        place_ = plane(1 - p if p < 2 else p, j % 4, x if j < 4 else 1 - x)
        return copy_to(place_, place_, xs.at[p, j], xr.at[p, j], across)

    def x_came(p, j):
        place_ = plane(p, j % 4, 1 - x if j < 4 else x)
        copy_to(place_, place_, xs.at[p, j], xr.at[p, j], across).wait_recv()

    def column(j):
        return j % 4, (x if j < 4 else 1 - x)

    def y_copy(p, j, whose):
        place_ = piece(p, *column(j), whose * half, half)
        return pltpu.make_async_remote_copy(
            src_ref=place_, dst_ref=place_, send_sem=ys.at[p, j], recv_sem=yr.at[p, j],
            device_id={"groups": 1 - group, "seq": me}, device_id_type=MESH,
        )

    def core_copy(p, j):
        place_ = piece(p, *column(j), 0, share)
        return copy_to(place_, place_, cs.at[p, j], cr.at[p, j], other)

    def own_core():
        place_ = w_buf.at[:, mine, :]
        return copy_to(place_, place_, os.at[0], orv.at[0], other)

    def own_core_came():
        start = pl.multiple_of(other * share, 16)
        place_ = w_buf.at[:, pl.ds(start, share), :]
        copy_to(place_, place_, os.at[0], orv.at[0], other).wait_recv()

    def take_z(q, j):
        z_came(q, j)
        p = (0, 0, 2, 3)[q]
        y_copy(p, j + 4 if q == 1 else j, group).start()
        x_copy(1 if q < 2 else q, j + 4 if q == 1 else j).start()

    def take_z_early(q, j):
        z_came(q, j)
        x_copy(q, j).start()

    def take_x(p, j):
        x_came(p, j)
        y_copy(p, j + 4 if j < 4 else j - 4, group).start()

    def take_y(p, j):
        y_copy(p, j, 1 - group).wait_recv()
        core_copy(p, j).start()

    def core_came(p):
        for j in swapped:
            place_ = w_buf.at[
                slots[p],
                pl.ds(pl.multiple_of(index(origin[j % 4], x if j < 4 else 1 - x, 1 - core) * share, 16), share),
                :,
            ]
            copy_to(place_, place_, cs.at[p, j], cr.at[p, j], other).wait_recv()

    swapped = (0, 1, 2, 4, 5, 6, 7)
    x_sent = ((0, 3),) + tuple((1, j) for j in range(7)) + tuple((p, j) for p in (2, 3) for j in range(4))
    m = acted_ref.shape[0]
    n = m // CHUNKS
    h = m // HALO

    def rows(i):
        return pl.ds(pl.multiple_of(i * n, n), n)

    def part_rows(i):
        return pl.ds(pl.multiple_of(i * h, h), h)

    def halo_z(i):
        r = part_rows(i)
        return copy_to(out_a.at[r, :], in_a.at[r, :], hzs.at[i], hzr.at[i], ahead)

    def halo_x(i):
        r = part_rows(i)
        return copy_to(out_s.at[r, :], in_s.at[r, :], hxs.at[i], hxr.at[i], across)

    tile = 64

    def act(i, carry):
        r = pl.ds(pl.multiple_of(i * tile, tile), tile)
        v = x_ref[r, :].astype(F32)
        t = jnp.tanh(COEF * (v + CUBE * v * v * v))
        acted_ref[r, :] = (0.5 * v * (1.0 + t)).astype(BF16)
        return carry

    def far_part(i, carry):
        out_a[rows(i), :] = jnp.dot(
            acted_ref[rows(i), :], w_buf[1 - x], preferred_element_type=F32
        ).astype(BF16)

        @pl.when(sends)
        def _():
            for k in range(HALO // CHUNKS):
                halo_z(i * (HALO // CHUNKS) + k).start()
        return carry

    def near_part(i, carry):
        part[rows(i), :] = jnp.dot(acted_ref[rows(i), :], w_buf[x], preferred_element_type=F32)
        return carry

    def combine(i):
        r = part_rows(i)

        @pl.when(takes)
        def _():
            halo_z(i).wait_recv()
            part[r, :] = part[r, :] + in_a[r, :].astype(F32)
        out_s[r, :] = part[r, :].astype(BF16)
        halo_x(i).start()

    def middle(i):
        part[rows(i), :] = jnp.dot(acted_ref[rows(i), :], w_buf[2], preferred_element_type=F32)
        gg[rows(i), :] = jnp.dot(cot_ref[rows(i), :], w_buf[3], preferred_element_type=F32)

    def finish(i):
        r = part_rows(i)
        halo_x(i).wait_recv()
        hidden = part[r, :] + in_s[r, :].astype(F32)
        value, slope = gelu_parts(hidden)
        gated_ref[r, :] = value.astype(BF16)
        hg_ref[r, :] = (gg[r, :] * slope).astype(BF16)
        back_x(i).start()

    wide = 4 * share
    wide_tile = 256
    hid = hg_ref.shape[1]
    chans = acted_ref.shape[1]
    even = x == 0
    back_sends = jnp.logical_or(jnp.logical_and(even, z < 3), jnp.logical_and(x == 1, z > 0))
    back_takes = jnp.logical_or(jnp.logical_and(even, z > 0), jnp.logical_and(x == 1, z < 3))
    back_ahead = index(lax.rem(z + (1 - 2 * x) + 4, 4), x, core)
    inside = jnp.logical_or(z == 1, z == 2)
    owner = (
        jnp.where(inside, origin[1], origin[2]), jnp.where(inside, origin[2], origin[1]), origin[0], z
    )

    def back_x(i):
        r = part_rows(i)
        return copy_to(hg_ref.at[r, :], near.at[0, r, :], bxs.at[i], bxr.at[i], across)

    def back_z(i):
        r = part_rows(i)
        return copy_to(near.at[0, r, :], near.at[1, r, :], bzs.at[i], bzr.at[i], back_ahead)

    def terms(s, j):
        return pl.ds(pl.multiple_of((2 * s + j) * share, share), share)

    def sum_core(s):
        return copy_to(give.at[s % 2], got.at[s % 2], rcs.at[s], rcr.at[s], other)

    def sum_x(s):
        return copy_to(x_out.at[s], x_in.at[s], rxs.at[s], rxr.at[s], across)

    def sum_z(s):
        p, k = s // 4, s % 4
        slot = jnp.where(inside, 0, 3) if k == 0 else k
        target = jnp.where(inside, origin[1], origin[0]) if k == 0 else owner[k]
        return copy_to(z_out.at[p * 3 + k], z_in.at[p * 4 + slot], rzs.at[p * 3 + k],
                       rzr.at[p * 4 + slot], index(target, x, core))

    def sum_came(p, slot):
        copy_to(z_out.at[0], z_in.at[p * 4 + slot], rzs.at[0], rzr.at[p * 4 + slot], across).wait_recv()

    def onward(i):
        back_x(i).wait_recv()

        @pl.when(back_sends)
        def _():
            back_z(i).start()

    def compute(s):
        if s >= 2:
            sum_core(s - 2).wait_send()
        cols = pl.ds(pl.multiple_of(owner[s % 4] * wide, wide), wide)
        for j, k in enumerate(PASSES[s // 4]):
            left = cot_ref if k == 3 else acted_ref

            def term(i, carry, k=k, j=j, left=left):
                t = pl.ds(pl.multiple_of(i * wide_tile, wide_tile), wide_tile)
                if k == 3:
                    right = gated_ref[:, t]
                elif k == 1:
                    right = hg_ref[:, t]
                else:
                    right = near[x if k == 0 else 1 - x, :, t]
                p = lax.dot_general(left[:, cols], right, TN, preferred_element_type=F32)
                for xx in range(2):
                    lo = p[2 * xx * share:(2 * xx + 1) * share]
                    hi = p[(2 * xx + 1) * share:(2 * xx + 2) * share]
                    keep[s % 2, xx, j, :, t] = jnp.where(core == 0, lo, hi)
                    give[s % 2, xx, j, :, t] = jnp.where(core == 0, hi, lo)
                return carry

            lax.fori_loop(0, hid // wide_tile, term, 0)
        if s >= 2:
            pl.semaphore_wait(free, 1)
        sum_core(s).start()

    def to_across(s):
        sum_core(s).wait_recv()

        def add(j, carry):
            x_out[s, j] = (keep[s % 2, 1 - x, j] + got[s % 2, 1 - x, j]).astype(BF16)
            sums[terms(s, j), :] = keep[s % 2, x, j] + got[s % 2, x, j]
            return carry

        lax.fori_loop(0, 2, add, 0)
        if s != 3:
            sum_x(s).start()
        if s < 6:
            pl.semaphore_signal(free, inc=1, device_id={"seq": other}, device_id_type=MESH)

    def to_z(s):
        p, k = s // 4, s % 4
        sum_x(s).wait_recv()

        def plain():
            for j in range(2):
                z_out[p * 3 + k, j] = (sums[terms(s, j), :] + x_in[s, j].astype(F32)).astype(BF16)

        if k == 1:
            pl.when(jnp.logical_not(inside))(plain)

            @pl.when(inside)
            def _():
                sum_came(p, 3)
                for j in range(2):
                    z_out[p * 3 + k, j] = (
                        sums[terms(s, j), :] + x_in[s, j].astype(F32) + z_in[p * 4 + 3, j].astype(F32)
                    ).astype(BF16)
        else:
            plain()
        sum_z(s).start()

    def total(p):
        s = 4 * p + 3
        sum_x(s).wait_recv()
        sum_came(p, 2)
        sum_came(p, 1)
        for j in range(2):
            own = sums[terms(s, j), :] + x_in[s, j].astype(F32)
            for slot in (1, 2):
                own = own + z_in[p * 4 + slot, j].astype(F32)
            grads_ref[PASSES[p][j]] = own * scale

        @pl.when(inside)
        def _():
            sum_came(p, 0)
            for j in range(2):
                t = PASSES[p][j]
                grads_ref[t] = grads_ref[t] + z_in[p * 4, j].astype(F32) * scale

    span = 512

    def project(i, carry):
        def span_part(j, c):
            t = pl.ds(pl.multiple_of(j * span, span), span)
            p = lax.dot_general(gated_ref[rows(i), :], w_buf[3, t, :], NT, preferred_element_type=F32)
            o_buf[rows(i), t] = (x_ref[rows(i), t].astype(F32) + p).astype(BF16)
            return c

        lax.fori_loop(0, chans // span, span_part, 0)
        return carry

    def spread(i, carry):
        def span_part(j, c):
            t = pl.ds(pl.multiple_of(j * span, span), span)
            p = lax.dot_general(hg_ref[rows(i), :], w_buf[2, t, :], NT, preferred_element_type=F32)
            p += lax.dot_general(near[x, rows(i), :], w_buf[0, t, :], NT, preferred_element_type=F32)
            p += lax.dot_general(near[1 - x, rows(i), :], w_buf[1, t, :], NT, preferred_element_type=F32)
            slope = gelu_parts(x_ref[rows(i), t].astype(F32))[1]
            g_buf[rows(i), t] = (cot_ref[rows(i), t].astype(F32) + p * slope).astype(BF16)
            return c

        lax.fori_loop(0, chans // span, span_part, 0)
        return carry

    for load in loads:
        load.wait()
    z_begin(0)
    x_copy(0, 3).start()
    own_core().start()
    x_copy(1, 3).start()
    x_load.wait()
    steps = m // tile
    lax.fori_loop(0, steps // 2, act, 0)
    take_x(0, 3)
    z_begin(1)
    lax.fori_loop(steps // 2, steps, act, 0)
    take_z(0, 0)
    take_z(0, 1)
    take_x(1, 3)
    take_z(0, 2)
    z_begin(2)
    z_begin(3)
    take_y(0, 7)
    take_x(1, 0)
    take_z(1, 0)
    take_y(0, 0)
    take_x(1, 1)
    take_z(1, 1)
    take_y(0, 1)
    take_x(1, 2)
    take_y(0, 2)
    take_z(1, 2)
    x_copy(2, 3).start()
    x_copy(3, 3).start()
    take_z_early(2, 0)
    take_y(0, 4)
    take_x(1, 4)
    take_y(0, 5)
    take_x(1, 5)
    take_z_early(2, 1)
    take_y(0, 6)
    own_core_came()
    core_came(0)
    lax.fori_loop(0, 2, far_part, 0)
    take_x(1, 6)
    y_copy(2, 0, group).start()
    y_copy(2, 1, group).start()
    lax.fori_loop(2, CHUNKS, far_part, 0)
    take_z(2, 2)
    take_x(2, 3)
    take_x(3, 3)
    take_y(1, 7)
    take_z(3, 0)
    take_y(1, 4)
    take_y(1, 5)
    take_x(2, 0)
    take_z(3, 1)
    take_y(1, 6)
    take_x(2, 1)
    take_y(1, 0)
    take_y(1, 1)
    take_z(3, 2)
    take_x(2, 2)
    take_y(1, 2)
    core_came(1)
    lax.fori_loop(0, CHUNKS, near_part, 0)
    take_x(3, 0)
    combine(0)
    take_x(3, 1)
    take_x(3, 2)
    for j in (0, 1, 2, 7):
        take_y(2, j)
    combine(1)
    for j in (4, 5, 6):
        take_y(2, j)
    combine(2)
    for j in (7, 0, 1, 4):
        take_y(3, j)
    combine(3)
    for j in (2, 5, 6):
        take_y(3, j)
    cot_load.wait()
    combine(4)
    core_came(2)
    core_came(3)
    middle(0)
    combine(5)
    middle(1)
    combine(6)
    middle(2)
    combine(7)
    middle(3)
    for i in range(HALO):
        finish(i)

    @pl.when(jnp.logical_not(back_takes))
    def _():
        near[1] = jnp.zeros((m, hid), BF16)

    project(0, 0)
    compute(0)
    onward(0)
    project(1, 0)
    onward(1)
    compute(1)
    to_across(0)
    onward(2)
    compute(2)
    onward(3)
    to_across(1)
    compute(3)
    onward(4)
    to_across(2)
    project(2, 0)
    project(3, 0)
    onward(5)
    to_across(3)
    onward(6)
    onward(7)

    @pl.when(back_takes)
    def _():
        for i in range(HALO):
            back_z(i).wait_recv()

    compute(4)
    to_z(0)
    compute(5)
    to_across(4)
    to_z(1)
    compute(6)
    to_across(5)
    to_z(2)
    compute(7)
    to_across(6)
    sum_x(3).start()
    to_across(7)
    spread(0, 0)
    to_z(4)
    spread(1, 0)
    spread(2, 0)
    to_z(5)
    to_z(6)
    spread(3, 0)
    total(0)
    total(1)
    own_core().wait_send()
    for q in range(4):
        for d in range(3):
            z_copy(q, d).wait_send()
    for p, j in x_sent:
        x_copy(p, j).wait_send()
    for p in range(4):
        for j in swapped:
            y_copy(p, j, group).wait_send()
            core_copy(p, j).wait_send()
    for i in range(HALO):
        halo_x(i).wait_send()
        back_x(i).wait_send()

    @pl.when(sends)
    def _():
        for i in range(HALO):
            halo_z(i).wait_send()

    @pl.when(back_sends)
    def _():
        for i in range(HALO):
            back_z(i).wait_send()

    sum_core(6).wait_send()
    sum_core(7).wait_send()
    for s in range(8):
        sum_x(s).wait_send()
        if s % 4 < 3:
            sum_z(s).wait_send()


def block(scale, conv_weight, proj_weight, flat, cot):
    share, hid = proj_weight.shape
    m, chans = flat.shape
    dma = pltpu.SemaphoreType.DMA
    pair = (2, 2, share, hid)
    halo = pltpu.VMEM((m, hid), BF16)
    wide = pltpu.VMEM((m, chans), BF16)
    return pl.pallas_call(
        functools.partial(block_kernel, scale),
        out_shape=(
            pltpu.VMEM((4, share, hid), F32), pltpu.VMEM((m, chans), BF16), pltpu.VMEM((m, chans), BF16),
        ),
        in_specs=[HBM] * 4,
        out_specs=(VMEM, VMEM, VMEM),
        scratch_shapes=[pltpu.VMEM((4, chans, hid), BF16), wide, wide, wide]
        + [halo] * 4 + [pltpu.VMEM((2 * m, hid), F32)] + [halo] * 2
        + [pltpu.VMEM((2, m, hid), BF16)]
        + [pltpu.VMEM((2,) + pair, F32)] * 3
        + [pltpu.VMEM((8, 2, share, hid), BF16)] * 2
        + [pltpu.VMEM((n, 2, share, hid), BF16) for n in (6, 8)]
        + [dma((8,)), dma((4, 3)), dma((4, 4))] + [dma((4, 8))] * 6
        + [dma((1,))] * 2 + [dma((HALO,))] * 8 + [dma((8,))] * 4 + [dma((6,)), dma((8,))]
        + [pltpu.SemaphoreType.REGULAR],
        compiler_params=params(1, 54),
        name="block_step",
    )(conv_weight, proj_weight, flat, cot)


def deliver_kernel(grads, outputs_in, input_grad_in, outputs, input_grad, conv, proj, gone):
    parts = 2
    m = outputs_in.shape[0] // parts
    moves = [(grads.at[pl.ds(0, 3)], conv), (grads.at[3], proj)]
    for i in range(parts):
        r = pl.ds(i * m, m)
        moves.append((outputs_in.at[r, :], outputs.at[r, :]))
        moves.append((input_grad_in.at[r, :], input_grad.at[r, :]))
    stores = [pltpu.make_async_copy(s, d, gone.at[i]) for i, (s, d) in enumerate(moves)]
    for store in stores:
        store.start()
    for store in stores:
        store.wait()


def deliver(grads, outputs, input_grad):
    like = lambda shape, kind: jax.ShapeDtypeStruct(shape, kind)
    return pl.pallas_call(
        deliver_kernel,
        out_shape=(
            like(outputs.shape, BF16), like(input_grad.shape, BF16),
            like((3,) + grads.shape[1:], F32), like(grads.shape[1:], F32),
        ),
        in_specs=[VMEM] * 3,
        out_specs=(HBM,) * 4,
        scratch_shapes=[pltpu.SemaphoreType.DMA((6,))],
        compiler_params=pltpu.CompilerParams(vmem_limit_bytes=2 * 1024 * 1024),
        name="deliver",
    )(grads, outputs, input_grad)


def pair_shards(inputs, conv_weight, proj_weight, cotangent):
    batch, local_len, chans = inputs.shape
    scale = 1.0 / float(batch * L) ** 0.5
    rows = inputs.reshape(-1, chans)
    cot = cotangent.reshape(-1, chans)
    outputs, input_grad, conv, proj = deliver(*block(scale, conv_weight, proj_weight, rows, cot))
    return (
        outputs.reshape(batch, local_len, chans),
        input_grad.reshape(batch, local_len, chans),
        conv.transpose(1, 0, 2),
        proj,
    )


def solution(mesh):
    fast = mesh.shape["seq"] == SEQ
    return jax.shard_map(
        pair_shards if fast else shards,
        mesh=mesh,
        in_specs=(
            P("groups", "seq", None),
            P(None, "seq", None),
            P("seq", None),
            P("groups", "seq", None),
        ),
        out_specs=(
            P("groups", "seq", None),
            P("groups", "seq", None),
            P(("groups", "seq"), None, None),
            P(("groups", "seq"), None),
        ),
        check_vma=False,
    )
```

```python
import functools

import jax
import jax.numpy as jnp
from jax import lax
from jax.experimental import pallas as pl
from jax.experimental.pallas import tpu as pltpu
from jax.sharding import PartitionSpec as P

L = 8192


def from_behind(block, axis, distance):
    devices = range(lax.axis_size(axis))
    route = [(i - distance, i) for i in devices if i - distance in devices]
    return lax.ppermute(block, axis, route)


def gelu_grad(point, upstream):
    return jax.vjp(jax.nn.gelu, point)[1](upstream)[0]


def shards(inputs, conv_weight, proj_weight, cotangent):
    batch, local_len, chans = inputs.shape
    devices = lax.axis_size("seq")
    stride = devices // 8
    scale = 1.0 / float(batch * L) ** 0.5
    acted = jax.nn.gelu(inputs.astype(jnp.float32)).astype(jnp.bfloat16)
    conv_weight, proj_weight = (
        lax.all_gather(conv_weight, "seq", axis=1, tiled=True),
        lax.all_gather(proj_weight, "seq", axis=0, tiled=True),
    )
    hid = conv_weight.shape[2]
    acted_rows = acted.reshape(-1, chans)
    before = from_behind(acted, "seq", stride)
    after = from_behind(acted, "seq", -stride)
    hidden = jnp.dot(before.reshape(-1, chans), conv_weight[0], preferred_element_type=jnp.float32)
    hidden = hidden + jnp.dot(acted_rows, conv_weight[1], preferred_element_type=jnp.float32)
    hidden = hidden + jnp.dot(
        after.reshape(-1, chans), conv_weight[2], preferred_element_type=jnp.float32
    )
    gated = jax.nn.gelu(hidden).astype(jnp.bfloat16)
    outputs = (
        inputs.reshape(-1, chans).astype(jnp.float32)
        + jnp.dot(gated, proj_weight.T, preferred_element_type=jnp.float32)
    ).astype(jnp.bfloat16)
    cot_rows = cotangent.reshape(-1, chans)
    gated_grad = jnp.dot(cot_rows, proj_weight, preferred_element_type=jnp.float32)
    hidden_grad = gelu_grad(hidden, gated_grad).astype(jnp.bfloat16)
    grad_blocks = hidden_grad.reshape(batch, local_len, hid)
    grad_later = from_behind(grad_blocks, "seq", -stride).reshape(-1, hid)
    grad_earlier = from_behind(grad_blocks, "seq", stride).reshape(-1, hid)
    acted_grad = jnp.dot(grad_later, conv_weight[0].T, preferred_element_type=jnp.float32)
    acted_grad = acted_grad + jnp.dot(
        hidden_grad, conv_weight[1].T, preferred_element_type=jnp.float32
    )
    acted_grad = acted_grad + jnp.dot(
        grad_earlier, conv_weight[2].T, preferred_element_type=jnp.float32
    )
    input_grad = (
        cot_rows.astype(jnp.float32)
        + gelu_grad(inputs.reshape(-1, chans).astype(jnp.float32), acted_grad)
    ).astype(jnp.bfloat16)
    tap_grads = (grad_later, hidden_grad, grad_earlier)
    share = chans // devices
    local_terms = [
        jnp.dot(acted_rows.T, piece, preferred_element_type=jnp.float32) for piece in tap_grads
    ]
    local_terms.append(jnp.dot(cot_rows.T, gated, preferred_element_type=jnp.float32))
    stacked = jnp.stack(local_terms, axis=1)
    received = lax.all_to_all(stacked, "seq", split_axis=0, concat_axis=0, tiled=True)
    summed = jnp.sum(received.reshape(devices, share, 4, received.shape[2]), axis=0)
    conv_sum = summed[:, 0:3, :]
    proj_sum = summed[:, 3, :]
    return (
        outputs.reshape(batch, local_len, chans),
        input_grad.reshape(batch, local_len, chans),
        conv_sum * scale,
        proj_sum * scale,
    )


F32 = jnp.float32
BF16 = jnp.bfloat16
MESH = pl.DeviceIdType.MESH
VMEM = pl.BlockSpec(memory_space=pltpu.VMEM)
HBM = pl.BlockSpec(memory_space=pl.ANY)
SEQ = 16
CHUNKS = 4
HALO = 8
COEF = 0.7978845608028654
CUBE = 0.044715


def place():
    s = lax.axis_index("seq")
    return s // 4, (s // 2) % 2, s % 2


def index(z, x, core):
    return (z * 2 + x) * 2 + core


def copy_to(src, dst, send, recv, target):
    return pltpu.make_async_remote_copy(
        src_ref=src, dst_ref=dst, send_sem=send, recv_sem=recv,
        device_id={"seq": target}, device_id_type=MESH,
    )


def gelu_parts(v):
    t = jnp.tanh(COEF * (v + CUBE * v * v * v))
    half = 0.5 * (1.0 + t)
    return half * v, half + (0.5 * COEF) * v * (1.0 - t * t) * (1.0 + (3.0 * CUBE) * v * v)


def params(cid, mib=56):
    return pltpu.CompilerParams(
        collective_id=cid, has_side_effects=True, vmem_limit_bytes=mib * 1024 * 1024
    )


PASSES = ((1, 3), (0, 2))
NT = (((1,), (1,)), ((), ()))
TN = (((0,), (0,)), ((), ()))


def block_kernel(scale, conv_hbm, proj_hbm, x_hbm, cot_hbm, grads_ref, o_buf, g_buf,
                 w_buf, x_ref, cot_ref, acted_ref, out_a, in_a, out_s, in_s, sums, gated_ref, hg_ref,
                 near, give, keep, got, x_out, x_in, z_out, z_in, own_sem,
                 zs, zr, xs, xr, ys, yr, cs, cr, os, orv, hzs, hzr, hxs, hxr,
                 bzs, bzr, bxs, bxr, rcs, rcr, rxs, rxr, rzs, rzr, free):
    z, x, core = place()
    group = lax.axis_index("groups")
    me = lax.axis_index("seq")
    share = proj_hbm.shape[0]
    across = index(z, 1 - x, core)
    other = index(z, x, 1 - core)
    origin = (z + 1 - 2 * lax.rem(z, 2), 2 - z // 2, 3 - 3 * (z // 2), z)
    up = x == 1
    sends = jnp.logical_or(jnp.logical_and(up, z < 3), jnp.logical_and(x == 0, z > 0))
    takes = jnp.logical_or(jnp.logical_and(up, z > 0), jnp.logical_and(x == 0, z < 3))
    ahead = index(lax.rem(z + (2 * x - 1) + 4, 4), x, core)

    mine = pl.ds(pl.multiple_of(me * share, share), share)
    loads = [
        pltpu.make_async_copy(conv_hbm.at[tap], w_buf.at[slot, mine, :], own_sem.at[slot])
        for slot, tap in enumerate((0, 2, 1))
    ]
    loads.append(pltpu.make_async_copy(proj_hbm, w_buf.at[3, mine, :], own_sem.at[3]))
    x_load = pltpu.make_async_copy(x_hbm, x_ref, own_sem.at[4])
    cot_load = pltpu.make_async_copy(cot_hbm, cot_ref, own_sem.at[5])
    for load in loads:
        load.start()
    x_load.start()
    cot_load.start()
    barrier = pltpu.get_barrier_semaphore()
    for target in [index(origin[j], x, core) for j in range(3)] + [across, other]:
        pl.semaphore_signal(barrier, inc=1, device_id={"seq": target}, device_id_type=MESH)
    pl.semaphore_signal(
        barrier, inc=1, device_id={"groups": 1 - group, "seq": me}, device_id_type=MESH
    )
    pl.semaphore_wait(barrier, 6)

    slots = (1 - x, x, 2, 3)
    part = sums.at[pl.ds(0, acted_ref.shape[0]), :]
    gg = sums.at[pl.ds(acted_ref.shape[0], acted_ref.shape[0]), :]
    half = share // 2
    inside = jnp.logical_or(z == 1, z == 2)

    def piece(p, j, xx, start, size):
        begin = pl.multiple_of(index(origin[j], xx, core) * share + start, 16)
        return w_buf.at[slots[p], pl.ds(begin, size), :]

    def plane(p, j, xx):
        return piece(p, j, xx, group * half, half)

    def z_piece(q, j):
        return plane((0, 0, 2, 3, 3)[q], j, 1 - x if q in (1, 4) else x)

    def z_copy(q, d):
        place_ = z_piece(q, 3)
        return copy_to(place_, place_, zs.at[q, d], zr.at[q, z], index(origin[d], x, core))

    def z_onward(q):
        place_ = z_piece(q, 2)
        return copy_to(place_, place_, zs.at[q, 3], zr.at[q, origin[2]], index(origin[0], x, core))

    def z_came(q, j):
        place_ = z_piece(q, j)
        copy_to(place_, place_, zs.at[q, 0], zr.at[q, origin[j]], across).wait_recv()
    def z_begin(q):
        z_copy(q, 0).start()
        z_copy(q, 1).start()
        if q < 2:
            z_copy(q, 2).start()
        else:
            @pl.when(inside)
            def _():
                z_copy(q, 2).start()

    def x_copy(p, j):
        place_ = plane(1 - p if p < 2 else p, j % 4, x if j < 4 else 1 - x)
        return copy_to(place_, place_, xs.at[p, j], xr.at[p, j], across)

    def x_came(p, j):
        place_ = plane(p, j % 4, 1 - x if j < 4 else x)
        copy_to(place_, place_, xs.at[p, j], xr.at[p, j], across).wait_recv()

    def column(j):
        return j % 4, (x if j < 4 else 1 - x)

    def y_copy(p, j, whose):
        place_ = piece(p, *column(j), whose * half, half)
        return pltpu.make_async_remote_copy(
            src_ref=place_, dst_ref=place_, send_sem=ys.at[p, j], recv_sem=yr.at[p, j],
            device_id={"groups": 1 - group, "seq": me}, device_id_type=MESH,
        )

    def core_copy(p, j):
        place_ = piece(p, *column(j), 0, share)
        return copy_to(place_, place_, cs.at[p, j], cr.at[p, j], other)

    def own_core():
        place_ = w_buf.at[:, mine, :]
        return copy_to(place_, place_, os.at[0], orv.at[0], other)

    def own_core_came():
        start = pl.multiple_of(other * share, 16)
        place_ = w_buf.at[:, pl.ds(start, share), :]
        copy_to(place_, place_, os.at[0], orv.at[0], other).wait_recv()

    def take_z(q, j):
        z_came(q, j)
        k = j + 4 if q in (1, 4) else j
        y_copy((0, 0, 2, 3, 3)[q], k, group).start()
        if q < 3:
            x_copy(1 if q < 2 else 2, k).start()

    def take_far(q, here):
        @pl.when(inside if here else jnp.logical_not(inside))
        def _():
            z_came(q, 2)
            if here:
                z_onward(q).start()
            k = 6 if q == 4 else 2
            if q == 2:
                x_copy(2, 2).start()
            y_copy(2 if q == 2 else 3, k, group).start()

    def take_z_early(q, j):
        z_came(q, j)
        x_copy(q, j).start()

    def take_x(p, j):
        x_came(p, j)
        y_copy(p, j + 4 if j < 4 else j - 4, group).start()

    def take_y(p, j):
        y_copy(p, j, 1 - group).wait_recv()
        core_copy(p, j).start()

    def core_came(p):
        for j in swapped:
            place_ = w_buf.at[
                slots[p],
                pl.ds(pl.multiple_of(index(origin[j % 4], x if j < 4 else 1 - x, 1 - core) * share, 16), share),
                :,
            ]
            copy_to(place_, place_, cs.at[p, j], cr.at[p, j], other).wait_recv()

    swapped = (0, 1, 2, 4, 5, 6, 7)
    x_sent = ((0, 3),) + tuple((1, j) for j in range(7)) + tuple((2, j) for j in range(4)) + ((3, 3),)
    m = acted_ref.shape[0]
    n = m // CHUNKS
    h = m // HALO

    def rows(i):
        return pl.ds(pl.multiple_of(i * n, n), n)

    def part_rows(i):
        return pl.ds(pl.multiple_of(i * h, h), h)

    def halo_z(i):
        r = part_rows(i)
        return copy_to(out_a.at[r, :], in_a.at[r, :], hzs.at[i], hzr.at[i], ahead)

    def halo_x(i):
        r = part_rows(i)
        return copy_to(out_s.at[r, :], in_s.at[r, :], hxs.at[i], hxr.at[i], across)

    tile = 64

    def act(i, carry):
        r = pl.ds(pl.multiple_of(i * tile, tile), tile)
        v = x_ref[r, :].astype(F32)
        t = jnp.tanh(COEF * (v + CUBE * v * v * v))
        acted_ref[r, :] = (0.5 * v * (1.0 + t)).astype(BF16)
        return carry

    def far_part(i, carry):
        out_a[rows(i), :] = jnp.dot(
            acted_ref[rows(i), :], w_buf[1 - x], preferred_element_type=F32
        ).astype(BF16)

        @pl.when(sends)
        def _():
            for k in range(HALO // CHUNKS):
                halo_z(i * (HALO // CHUNKS) + k).start()
        return carry

    def near_part(i, carry):
        part[rows(i), :] = jnp.dot(acted_ref[rows(i), :], w_buf[x], preferred_element_type=F32)
        return carry

    def combine(i):
        r = part_rows(i)

        @pl.when(takes)
        def _():
            halo_z(i).wait_recv()
            part[r, :] = part[r, :] + in_a[r, :].astype(F32)
        out_s[r, :] = part[r, :].astype(BF16)
        halo_x(i).start()

    def middle(i):
        part[rows(i), :] = jnp.dot(acted_ref[rows(i), :], w_buf[2], preferred_element_type=F32)
        gg[rows(i), :] = jnp.dot(cot_ref[rows(i), :], w_buf[3], preferred_element_type=F32)

    def finish(i):
        r = part_rows(i)
        halo_x(i).wait_recv()
        hidden = part[r, :] + in_s[r, :].astype(F32)
        value, slope = gelu_parts(hidden)
        gated_ref[r, :] = value.astype(BF16)
        hg_ref[r, :] = (gg[r, :] * slope).astype(BF16)
        back_x(i).start()

    wide = 4 * share
    wide_tile = 256
    hid = hg_ref.shape[1]
    chans = acted_ref.shape[1]
    even = x == 0
    back_sends = jnp.logical_or(jnp.logical_and(even, z < 3), jnp.logical_and(x == 1, z > 0))
    back_takes = jnp.logical_or(jnp.logical_and(even, z > 0), jnp.logical_and(x == 1, z < 3))
    back_ahead = index(lax.rem(z + (1 - 2 * x) + 4, 4), x, core)
    owner = (
        jnp.where(inside, origin[1], origin[2]), jnp.where(inside, origin[2], origin[1]), origin[0], z
    )

    def back_x(i):
        r = part_rows(i)
        return copy_to(hg_ref.at[r, :], near.at[0, r, :], bxs.at[i], bxr.at[i], across)

    def back_z(i):
        r = part_rows(i)
        return copy_to(near.at[0, r, :], near.at[1, r, :], bzs.at[i], bzr.at[i], back_ahead)

    def terms(s, j):
        return pl.ds(pl.multiple_of((2 * s + j) * share, share), share)

    def sum_core(s):
        return copy_to(give.at[s % 2], got.at[s % 2], rcs.at[s], rcr.at[s], other)

    def sum_x(s):
        return copy_to(x_out.at[s], x_in.at[s], rxs.at[s], rxr.at[s], across)

    def sum_z(s):
        p, k = s // 4, s % 4
        slot = jnp.where(inside, 0, 3) if k == 0 else k
        target = jnp.where(inside, origin[1], origin[0]) if k == 0 else owner[k]
        return copy_to(z_out.at[p * 3 + k], z_in.at[p * 4 + slot], rzs.at[p * 3 + k],
                       rzr.at[p * 4 + slot], index(target, x, core))

    def sum_came(p, slot):
        copy_to(z_out.at[0], z_in.at[p * 4 + slot], rzs.at[0], rzr.at[p * 4 + slot], across).wait_recv()

    def onward(i):
        back_x(i).wait_recv()

        @pl.when(back_sends)
        def _():
            back_z(i).start()

    def compute(s):
        if s >= 2:
            sum_core(s - 2).wait_send()
        cols = pl.ds(pl.multiple_of(owner[s % 4] * wide, wide), wide)
        for j, k in enumerate(PASSES[s // 4]):
            left = cot_ref if k == 3 else acted_ref

            def term(i, carry, k=k, j=j, left=left):
                t = pl.ds(pl.multiple_of(i * wide_tile, wide_tile), wide_tile)
                if k == 3:
                    right = gated_ref[:, t]
                elif k == 1:
                    right = hg_ref[:, t]
                else:
                    right = near[x if k == 0 else 1 - x, :, t]
                p = lax.dot_general(left[:, cols], right, TN, preferred_element_type=F32)
                for xx in range(2):
                    lo = p[2 * xx * share:(2 * xx + 1) * share]
                    hi = p[(2 * xx + 1) * share:(2 * xx + 2) * share]
                    keep[s % 2, xx, j, :, t] = jnp.where(core == 0, lo, hi)
                    give[s % 2, xx, j, :, t] = jnp.where(core == 0, hi, lo)
                return carry

            lax.fori_loop(0, hid // wide_tile, term, 0)
        if s >= 2:
            pl.semaphore_wait(free, 1)
        sum_core(s).start()

    def to_across(s):
        sum_core(s).wait_recv()

        def add(j, carry):
            x_out[s, j] = (keep[s % 2, 1 - x, j] + got[s % 2, 1 - x, j]).astype(BF16)
            sums[terms(s, j), :] = keep[s % 2, x, j] + got[s % 2, x, j]
            return carry

        lax.fori_loop(0, 2, add, 0)
        if s != 3:
            sum_x(s).start()
        if s < 6:
            pl.semaphore_signal(free, inc=1, device_id={"seq": other}, device_id_type=MESH)

    def to_z(s):
        p, k = s // 4, s % 4
        sum_x(s).wait_recv()

        def plain():
            for j in range(2):
                z_out[p * 3 + k, j] = (sums[terms(s, j), :] + x_in[s, j].astype(F32)).astype(BF16)

        if k == 1:
            pl.when(jnp.logical_not(inside))(plain)

            @pl.when(inside)
            def _():
                sum_came(p, 3)
                for j in range(2):
                    z_out[p * 3 + k, j] = (
                        sums[terms(s, j), :] + x_in[s, j].astype(F32) + z_in[p * 4 + 3, j].astype(F32)
                    ).astype(BF16)
        else:
            plain()
        sum_z(s).start()

    def total(p):
        s = 4 * p + 3
        sum_x(s).wait_recv()
        sum_came(p, 2)
        sum_came(p, 1)
        for j in range(2):
            own = sums[terms(s, j), :] + x_in[s, j].astype(F32)
            for slot in (1, 2):
                own = own + z_in[p * 4 + slot, j].astype(F32)
            grads_ref[PASSES[p][j]] = own * scale

        @pl.when(inside)
        def _():
            sum_came(p, 0)
            for j in range(2):
                t = PASSES[p][j]
                grads_ref[t] = grads_ref[t] + z_in[p * 4, j].astype(F32) * scale

    span = 512

    def project(i, carry):
        def span_part(j, c):
            t = pl.ds(pl.multiple_of(j * span, span), span)
            p = lax.dot_general(gated_ref[rows(i), :], w_buf[3, t, :], NT, preferred_element_type=F32)
            o_buf[rows(i), t] = (x_ref[rows(i), t].astype(F32) + p).astype(BF16)
            return c

        lax.fori_loop(0, chans // span, span_part, 0)
        return carry

    def spread(i, carry):
        def span_part(j, c):
            t = pl.ds(pl.multiple_of(j * span, span), span)
            p = lax.dot_general(hg_ref[rows(i), :], w_buf[2, t, :], NT, preferred_element_type=F32)
            p += lax.dot_general(near[x, rows(i), :], w_buf[0, t, :], NT, preferred_element_type=F32)
            p += lax.dot_general(near[1 - x, rows(i), :], w_buf[1, t, :], NT, preferred_element_type=F32)
            slope = gelu_parts(x_ref[rows(i), t].astype(F32))[1]
            g_buf[rows(i), t] = (cot_ref[rows(i), t].astype(F32) + p * slope).astype(BF16)
            return c

        lax.fori_loop(0, chans // span, span_part, 0)
        return carry

    for load in loads:
        load.wait()
    z_begin(0)
    x_copy(0, 3).start()
    own_core().start()
    x_copy(1, 3).start()
    x_copy(2, 3).start()
    x_copy(3, 3).start()
    x_load.wait()
    steps = m // tile
    lax.fori_loop(0, steps // 2, act, 0)
    take_x(0, 3)
    z_begin(1)
    lax.fori_loop(steps // 2, steps, act, 0)
    take_z(0, 0)
    take_z(0, 1)
    take_x(1, 3)
    take_z(0, 2)
    z_begin(2)
    z_begin(3)
    x_came(3, 3)
    z_begin(4)
    take_y(0, 7)
    take_x(1, 0)
    take_z(1, 0)
    take_y(0, 0)
    take_x(1, 1)
    take_z(1, 1)
    take_y(0, 1)
    take_x(1, 2)
    take_y(0, 2)
    take_z(1, 2)
    take_z_early(2, 0)
    take_y(0, 4)
    take_x(1, 4)
    take_y(0, 5)
    take_x(1, 5)
    take_z_early(2, 1)
    take_y(0, 6)
    own_core_came()
    core_came(0)
    take_far(2, True)
    lax.fori_loop(0, 2, far_part, 0)
    take_x(1, 6)
    y_copy(2, 0, group).start()
    y_copy(2, 1, group).start()
    take_x(2, 3)
    take_y(1, 7)
    take_y(1, 4)
    take_y(1, 5)
    take_x(2, 0)
    take_y(1, 6)
    take_x(2, 1)
    take_far(3, True)
    take_y(1, 0)
    take_y(1, 1)
    take_y(1, 2)
    y_copy(3, 7, group).start()
    core_came(1)
    take_far(4, True)
    lax.fori_loop(0, 2, near_part, 0)
    combine(0)
    lax.fori_loop(2, CHUNKS, near_part, 0)
    lax.fori_loop(2, CHUNKS, far_part, 0)
    take_far(2, False)
    take_z(3, 0)
    combine(1)
    take_x(2, 2)
    take_z(3, 1)
    take_z(4, 0)
    for j in (0, 1, 7, 4):
        take_y(2, j)
    combine(2)
    take_z(4, 1)
    for j in (5, 2, 6):
        take_y(2, j)
    combine(3)
    take_far(3, False)
    take_far(4, False)
    for j in (7, 0, 1, 4):
        take_y(3, j)
    combine(4)
    for j in (5, 2, 6):
        take_y(3, j)
    cot_load.wait()
    core_came(2)
    core_came(3)
    middle(0)
    combine(5)
    middle(1)
    combine(6)
    middle(2)
    combine(7)
    middle(3)
    for i in range(HALO):
        finish(i)

    @pl.when(jnp.logical_not(back_takes))
    def _():
        near[1] = jnp.zeros((m, hid), BF16)

    project(0, 0)
    compute(0)
    onward(0)
    project(1, 0)
    onward(1)
    compute(1)
    to_across(0)
    onward(2)
    compute(2)
    onward(3)
    to_across(1)
    compute(3)
    onward(4)
    to_across(2)
    project(2, 0)
    project(3, 0)
    onward(5)
    to_across(3)
    onward(6)
    onward(7)

    @pl.when(back_takes)
    def _():
        for i in range(HALO):
            back_z(i).wait_recv()

    compute(4)
    to_z(0)
    compute(5)
    to_across(4)
    to_z(1)
    compute(6)
    to_across(5)
    to_z(2)
    compute(7)
    to_across(6)
    sum_x(3).start()
    to_across(7)
    spread(0, 0)
    to_z(4)
    spread(1, 0)
    spread(2, 0)
    to_z(5)
    to_z(6)
    spread(3, 0)
    total(0)
    total(1)
    own_core().wait_send()
    for q in range(5):
        for d in range(3 if q < 2 else 2):
            z_copy(q, d).wait_send()

    @pl.when(inside)
    def _():
        for q in (2, 3, 4):
            z_copy(q, 2).wait_send()
            z_onward(q).wait_send()

    for p, j in x_sent:
        x_copy(p, j).wait_send()
    for p in range(4):
        for j in swapped:
            y_copy(p, j, group).wait_send()
            core_copy(p, j).wait_send()
    for i in range(HALO):
        halo_x(i).wait_send()
        back_x(i).wait_send()

    @pl.when(sends)
    def _():
        for i in range(HALO):
            halo_z(i).wait_send()

    @pl.when(back_sends)
    def _():
        for i in range(HALO):
            back_z(i).wait_send()

    sum_core(6).wait_send()
    sum_core(7).wait_send()
    for s in range(8):
        sum_x(s).wait_send()
        if s % 4 < 3:
            sum_z(s).wait_send()


def block(scale, conv_weight, proj_weight, flat, cot):
    share, hid = proj_weight.shape
    m, chans = flat.shape
    dma = pltpu.SemaphoreType.DMA
    pair = (2, 2, share, hid)
    halo = pltpu.VMEM((m, hid), BF16)
    wide = pltpu.VMEM((m, chans), BF16)
    return pl.pallas_call(
        functools.partial(block_kernel, scale),
        out_shape=(
            pltpu.VMEM((4, share, hid), F32), pltpu.VMEM((m, chans), BF16), pltpu.VMEM((m, chans), BF16),
        ),
        in_specs=[HBM] * 4,
        out_specs=(VMEM, VMEM, VMEM),
        scratch_shapes=[pltpu.VMEM((4, chans, hid), BF16), wide, wide, wide]
        + [halo] * 4 + [pltpu.VMEM((2 * m, hid), F32)] + [halo] * 2
        + [pltpu.VMEM((2, m, hid), BF16)]
        + [pltpu.VMEM((2,) + pair, F32)] * 3
        + [pltpu.VMEM((8, 2, share, hid), BF16)] * 2
        + [pltpu.VMEM((n, 2, share, hid), BF16) for n in (6, 8)]
        + [dma((8,)), dma((5, 4)), dma((5, 4))] + [dma((4, 8))] * 6
        + [dma((1,))] * 2 + [dma((HALO,))] * 8 + [dma((8,))] * 4 + [dma((6,)), dma((8,))]
        + [pltpu.SemaphoreType.REGULAR],
        compiler_params=params(1, 54),
        name="block_step",
    )(conv_weight, proj_weight, flat, cot)


def deliver_kernel(grads, outputs_in, input_grad_in, outputs, input_grad, conv, proj, gone):
    parts = 2
    m = outputs_in.shape[0] // parts
    moves = [(grads.at[pl.ds(0, 3)], conv), (grads.at[3], proj)]
    for i in range(parts):
        r = pl.ds(i * m, m)
        moves.append((outputs_in.at[r, :], outputs.at[r, :]))
        moves.append((input_grad_in.at[r, :], input_grad.at[r, :]))
    stores = [pltpu.make_async_copy(s, d, gone.at[i]) for i, (s, d) in enumerate(moves)]
    for store in stores:
        store.start()
    for store in stores:
        store.wait()


def deliver(grads, outputs, input_grad):
    like = lambda shape, kind: jax.ShapeDtypeStruct(shape, kind)
    return pl.pallas_call(
        deliver_kernel,
        out_shape=(
            like(outputs.shape, BF16), like(input_grad.shape, BF16),
            like((3,) + grads.shape[1:], F32), like(grads.shape[1:], F32),
        ),
        in_specs=[VMEM] * 3,
        out_specs=(HBM,) * 4,
        scratch_shapes=[pltpu.SemaphoreType.DMA((6,))],
        compiler_params=pltpu.CompilerParams(vmem_limit_bytes=2 * 1024 * 1024),
        name="deliver",
    )(grads, outputs, input_grad)


def pair_shards(inputs, conv_weight, proj_weight, cotangent):
    batch, local_len, chans = inputs.shape
    scale = 1.0 / float(batch * L) ** 0.5
    rows = inputs.reshape(-1, chans)
    cot = cotangent.reshape(-1, chans)
    outputs, input_grad, conv, proj = deliver(*block(scale, conv_weight, proj_weight, rows, cot))
    return (
        outputs.reshape(batch, local_len, chans),
        input_grad.reshape(batch, local_len, chans),
        conv.transpose(1, 0, 2),
        proj,
    )


def solution(mesh):
    fast = mesh.shape["seq"] == SEQ
    return jax.shard_map(
        pair_shards if fast else shards,
        mesh=mesh,
        in_specs=(
            P("groups", "seq", None),
            P(None, "seq", None),
            P("seq", None),
            P("groups", "seq", None),
        ),
        out_specs=(
            P("groups", "seq", None),
            P("groups", "seq", None),
            P(("groups", "seq"), None, None),
            P(("groups", "seq"), None),
        ),
        check_vma=False,
    )
```

```python
import functools

import jax
import jax.numpy as jnp
from jax import lax
from jax.experimental import pallas as pl
from jax.experimental.pallas import tpu as pltpu
from jax.sharding import PartitionSpec as P

L = 8192


def from_behind(block, axis, distance):
    devices = range(lax.axis_size(axis))
    route = [(i - distance, i) for i in devices if i - distance in devices]
    return lax.ppermute(block, axis, route)


def gelu_grad(point, upstream):
    return jax.vjp(jax.nn.gelu, point)[1](upstream)[0]


def shards(inputs, conv_weight, proj_weight, cotangent):
    batch, local_len, chans = inputs.shape
    devices = lax.axis_size("seq")
    stride = devices // 8
    scale = 1.0 / float(batch * L) ** 0.5
    acted = jax.nn.gelu(inputs.astype(jnp.float32)).astype(jnp.bfloat16)
    conv_weight, proj_weight = (
        lax.all_gather(conv_weight, "seq", axis=1, tiled=True),
        lax.all_gather(proj_weight, "seq", axis=0, tiled=True),
    )
    hid = conv_weight.shape[2]
    acted_rows = acted.reshape(-1, chans)
    before = from_behind(acted, "seq", stride)
    after = from_behind(acted, "seq", -stride)
    hidden = jnp.dot(before.reshape(-1, chans), conv_weight[0], preferred_element_type=jnp.float32)
    hidden = hidden + jnp.dot(acted_rows, conv_weight[1], preferred_element_type=jnp.float32)
    hidden = hidden + jnp.dot(
        after.reshape(-1, chans), conv_weight[2], preferred_element_type=jnp.float32
    )
    gated = jax.nn.gelu(hidden).astype(jnp.bfloat16)
    outputs = (
        inputs.reshape(-1, chans).astype(jnp.float32)
        + jnp.dot(gated, proj_weight.T, preferred_element_type=jnp.float32)
    ).astype(jnp.bfloat16)
    cot_rows = cotangent.reshape(-1, chans)
    gated_grad = jnp.dot(cot_rows, proj_weight, preferred_element_type=jnp.float32)
    hidden_grad = gelu_grad(hidden, gated_grad).astype(jnp.bfloat16)
    grad_blocks = hidden_grad.reshape(batch, local_len, hid)
    grad_later = from_behind(grad_blocks, "seq", -stride).reshape(-1, hid)
    grad_earlier = from_behind(grad_blocks, "seq", stride).reshape(-1, hid)
    acted_grad = jnp.dot(grad_later, conv_weight[0].T, preferred_element_type=jnp.float32)
    acted_grad = acted_grad + jnp.dot(
        hidden_grad, conv_weight[1].T, preferred_element_type=jnp.float32
    )
    acted_grad = acted_grad + jnp.dot(
        grad_earlier, conv_weight[2].T, preferred_element_type=jnp.float32
    )
    input_grad = (
        cot_rows.astype(jnp.float32)
        + gelu_grad(inputs.reshape(-1, chans).astype(jnp.float32), acted_grad)
    ).astype(jnp.bfloat16)
    tap_grads = (grad_later, hidden_grad, grad_earlier)
    share = chans // devices
    local_terms = [
        jnp.dot(acted_rows.T, piece, preferred_element_type=jnp.float32) for piece in tap_grads
    ]
    local_terms.append(jnp.dot(cot_rows.T, gated, preferred_element_type=jnp.float32))
    stacked = jnp.stack(local_terms, axis=1)
    received = lax.all_to_all(stacked, "seq", split_axis=0, concat_axis=0, tiled=True)
    summed = jnp.sum(received.reshape(devices, share, 4, received.shape[2]), axis=0)
    conv_sum = summed[:, 0:3, :]
    proj_sum = summed[:, 3, :]
    return (
        outputs.reshape(batch, local_len, chans),
        input_grad.reshape(batch, local_len, chans),
        conv_sum * scale,
        proj_sum * scale,
    )


F32 = jnp.float32
BF16 = jnp.bfloat16
MESH = pl.DeviceIdType.MESH
VMEM = pl.BlockSpec(memory_space=pltpu.VMEM)
HBM = pl.BlockSpec(memory_space=pl.ANY)
SEQ = 16
CHUNKS = 4
HALO = 8
COEF = 0.7978845608028654
CUBE = 0.044715


def place():
    s = lax.axis_index("seq")
    return s // 4, (s // 2) % 2, s % 2


def index(z, x, core):
    return (z * 2 + x) * 2 + core


def copy_to(src, dst, send, recv, target):
    return pltpu.make_async_remote_copy(
        src_ref=src, dst_ref=dst, send_sem=send, recv_sem=recv,
        device_id={"seq": target}, device_id_type=MESH,
    )


def gelu_parts(v):
    t = jnp.tanh(COEF * (v + CUBE * v * v * v))
    half = 0.5 * (1.0 + t)
    return half * v, half + (0.5 * COEF) * v * (1.0 - t * t) * (1.0 + (3.0 * CUBE) * v * v)


def params(cid, mib=56):
    return pltpu.CompilerParams(
        collective_id=cid, has_side_effects=True, vmem_limit_bytes=mib * 1024 * 1024
    )


PASSES = ((1, 3), (0, 2))
NT = (((1,), (1,)), ((), ()))
TN = (((0,), (0,)), ((), ()))


def block_kernel(scale, conv_hbm, proj_hbm, x_hbm, cot_hbm, grads_ref, o_buf, g_buf,
                 w_buf, x_ref, cot_ref, acted_ref, out_a, in_a, out_s, in_s, sums, gated_ref, hg_ref,
                 near, give, keep, got, x_out, x_in, z_out, z_in, own_sem,
                 zs, zr, xs, xr, ys, yr, cs, cr, os, orv, hzs, hzr, hxs, hxr,
                 bzs, bzr, bxs, bxr, rcs, rcr, rxs, rxr, rzs, rzr, free):
    z, x, core = place()
    group = lax.axis_index("groups")
    me = lax.axis_index("seq")
    share = proj_hbm.shape[0]
    across = index(z, 1 - x, core)
    other = index(z, x, 1 - core)
    origin = (z + 1 - 2 * lax.rem(z, 2), 2 - z // 2, 3 - 3 * (z // 2), z)
    up = x == 1
    sends = jnp.logical_or(jnp.logical_and(up, z < 3), jnp.logical_and(x == 0, z > 0))
    takes = jnp.logical_or(jnp.logical_and(up, z > 0), jnp.logical_and(x == 0, z < 3))
    ahead = index(lax.rem(z + (2 * x - 1) + 4, 4), x, core)

    mine = pl.ds(pl.multiple_of(me * share, share), share)
    loads = [
        pltpu.make_async_copy(conv_hbm.at[tap], w_buf.at[slot, mine, :], own_sem.at[slot])
        for slot, tap in enumerate((0, 2, 1))
    ]
    loads.append(pltpu.make_async_copy(proj_hbm, w_buf.at[3, mine, :], own_sem.at[3]))
    x_load = pltpu.make_async_copy(x_hbm, x_ref, own_sem.at[4])
    cot_load = pltpu.make_async_copy(cot_hbm, cot_ref, own_sem.at[5])
    for load in loads:
        load.start()
    x_load.start()
    cot_load.start()
    barrier = pltpu.get_barrier_semaphore()
    for target in [index(origin[j], x, core) for j in range(3)] + [across, other]:
        pl.semaphore_signal(barrier, inc=1, device_id={"seq": target}, device_id_type=MESH)
    pl.semaphore_signal(
        barrier, inc=1, device_id={"groups": 1 - group, "seq": me}, device_id_type=MESH
    )
    pl.semaphore_wait(barrier, 6)

    slots = (1 - x, x, 2, 3)
    part = sums.at[pl.ds(0, acted_ref.shape[0]), :]
    gg = sums.at[pl.ds(acted_ref.shape[0], acted_ref.shape[0]), :]
    half = share // 2
    inside = jnp.logical_or(z == 1, z == 2)

    def piece(p, j, xx, start, size):
        begin = pl.multiple_of(index(origin[j], xx, core) * share + start, 16)
        return w_buf.at[slots[p], pl.ds(begin, size), :]

    def plane(p, j, xx):
        return piece(p, j, xx, group * half, half)

    def z_piece(q, j):
        return plane((0, 0, 2, 3, 3)[q], j, 1 - x if q in (1, 4) else x)

    def z_copy(q, d):
        place_ = z_piece(q, 3)
        return copy_to(place_, place_, zs.at[q, d], zr.at[q, z], index(origin[d], x, core))

    def z_onward(q):
        place_ = z_piece(q, 2)
        return copy_to(place_, place_, zs.at[q, 3], zr.at[q, origin[2]], index(origin[0], x, core))

    def z_came(q, j):
        place_ = z_piece(q, j)
        copy_to(place_, place_, zs.at[q, 0], zr.at[q, origin[j]], across).wait_recv()
    def z_begin(q):
        z_copy(q, 0).start()
        z_copy(q, 1).start()

        @pl.when(inside)
        def _():
            z_copy(q, 2).start()

    def x_copy(p, j):
        if (p, j) == (1, 3):
            place_ = piece(0, 3, x, 0, share)
        else:
            place_ = plane(1 - p if p < 2 else p, j % 4, x if j < 4 else 1 - x)
        return copy_to(place_, place_, xs.at[p, j], xr.at[p, j], across)

    def x_came(p, j):
        if (p, j) == (1, 3):
            place_ = piece(1, 3, 1 - x, 0, share)
        else:
            place_ = plane(p, j % 4, 1 - x if j < 4 else x)
        copy_to(place_, place_, xs.at[p, j], xr.at[p, j], across).wait_recv()

    def column(j):
        return j % 4, (x if j < 4 else 1 - x)

    def y_copy(p, j, whose):
        place_ = piece(p, *column(j), whose * half, half)
        return pltpu.make_async_remote_copy(
            src_ref=place_, dst_ref=place_, send_sem=ys.at[p, j], recv_sem=yr.at[p, j],
            device_id={"groups": 1 - group, "seq": me}, device_id_type=MESH,
        )

    def core_copy(p, j):
        place_ = piece(p, *column(j), 0, share)
        return copy_to(place_, place_, cs.at[p, j], cr.at[p, j], other)

    def own_core():
        place_ = w_buf.at[:, mine, :]
        return copy_to(place_, place_, os.at[0], orv.at[0], other)

    def own_core_came():
        start = pl.multiple_of(other * share, 16)
        place_ = w_buf.at[:, pl.ds(start, share), :]
        copy_to(place_, place_, os.at[0], orv.at[0], other).wait_recv()

    def take_z(q, j):
        z_came(q, j)
        k = j + 4 if q in (1, 4) else j
        y_copy((0, 0, 2, 3, 3)[q], k, group).start()
        if q < 3:
            x_copy(1 if q < 2 else 2, k).start()

    def take_far(q, here):
        @pl.when(inside if here else jnp.logical_not(inside))
        def _():
            z_came(q, 2)
            if here:
                z_onward(q).start()
            k = 6 if q in (1, 4) else 2
            if q < 3:
                x_copy(1 if q < 2 else 2, k).start()
            y_copy((0, 0, 2, 3, 3)[q], k, group).start()

    def take_z_early(q, j):
        z_came(q, j)
        x_copy(q, j).start()

    def take_x(p, j):
        x_came(p, j)
        y_copy(p, j + 4 if j < 4 else j - 4, group).start()

    def take_y(p, j):
        y_copy(p, j, 1 - group).wait_recv()
        core_copy(p, j).start()

    def core_came(p):
        for j in swapped:
            place_ = w_buf.at[
                slots[p],
                pl.ds(pl.multiple_of(index(origin[j % 4], x if j < 4 else 1 - x, 1 - core) * share, 16), share),
                :,
            ]
            copy_to(place_, place_, cs.at[p, j], cr.at[p, j], other).wait_recv()

    swapped = (0, 1, 2, 4, 5, 6, 7)
    x_sent = ((0, 3),) + tuple((1, j) for j in range(7)) + tuple((2, j) for j in range(4)) + ((3, 3),)
    m = acted_ref.shape[0]
    n = m // CHUNKS
    h = m // HALO

    def rows(i):
        return pl.ds(pl.multiple_of(i * n, n), n)

    def part_rows(i):
        return pl.ds(pl.multiple_of(i * h, h), h)

    def halo_z(i):
        r = part_rows(i)
        return copy_to(out_a.at[r, :], in_a.at[r, :], hzs.at[i], hzr.at[i], ahead)

    def halo_x(i):
        r = part_rows(i)
        return copy_to(out_s.at[r, :], in_s.at[r, :], hxs.at[i], hxr.at[i], across)

    tile = 64

    def act(i, carry):
        r = pl.ds(pl.multiple_of(i * tile, tile), tile)
        v = x_ref[r, :].astype(F32)
        t = jnp.tanh(COEF * (v + CUBE * v * v * v))
        acted_ref[r, :] = (0.5 * v * (1.0 + t)).astype(BF16)
        return carry

    def far_part(i, carry):
        out_a[rows(i), :] = jnp.dot(
            acted_ref[rows(i), :], w_buf[1 - x], preferred_element_type=F32
        ).astype(BF16)

        @pl.when(sends)
        def _():
            for k in range(HALO // CHUNKS):
                halo_z(i * (HALO // CHUNKS) + k).start()
        return carry

    def near_part(i, carry):
        part[rows(i), :] = jnp.dot(acted_ref[rows(i), :], w_buf[x], preferred_element_type=F32)
        return carry

    def combine(i):
        r = part_rows(i)

        @pl.when(takes)
        def _():
            halo_z(i).wait_recv()
            part[r, :] = part[r, :] + in_a[r, :].astype(F32)
        out_s[r, :] = part[r, :].astype(BF16)
        halo_x(i).start()

    def middle(i):
        part[rows(i), :] = jnp.dot(acted_ref[rows(i), :], w_buf[2], preferred_element_type=F32)
        gg[rows(i), :] = jnp.dot(cot_ref[rows(i), :], w_buf[3], preferred_element_type=F32)

    def finish(i):
        r = part_rows(i)
        halo_x(i).wait_recv()
        hidden = part[r, :] + in_s[r, :].astype(F32)
        value, slope = gelu_parts(hidden)
        gated_ref[r, :] = value.astype(BF16)
        hg_ref[r, :] = (gg[r, :] * slope).astype(BF16)
        back_x(i).start()

    wide = 4 * share
    wide_tile = 256
    hid = hg_ref.shape[1]
    chans = acted_ref.shape[1]
    even = x == 0
    back_sends = jnp.logical_or(jnp.logical_and(even, z < 3), jnp.logical_and(x == 1, z > 0))
    back_takes = jnp.logical_or(jnp.logical_and(even, z > 0), jnp.logical_and(x == 1, z < 3))
    back_ahead = index(lax.rem(z + (1 - 2 * x) + 4, 4), x, core)
    owner = (
        jnp.where(inside, origin[1], origin[2]), jnp.where(inside, origin[2], origin[1]), origin[0], z
    )

    def back_x(i):
        r = part_rows(i)
        return copy_to(hg_ref.at[r, :], near.at[0, r, :], bxs.at[i], bxr.at[i], across)

    def back_z(i):
        r = part_rows(i)
        return copy_to(near.at[0, r, :], near.at[1, r, :], bzs.at[i], bzr.at[i], back_ahead)

    def terms(s, j):
        return pl.ds(pl.multiple_of((2 * s + j) * share, share), share)

    def sum_core(s):
        return copy_to(give.at[s % 2], got.at[s % 2], rcs.at[s], rcr.at[s], other)

    def sum_x(s):
        return copy_to(x_out.at[s], x_in.at[s], rxs.at[s], rxr.at[s], across)

    def sum_z(s):
        p, k = s // 4, s % 4
        slot = jnp.where(inside, 0, 3) if k == 0 else k
        target = jnp.where(inside, origin[1], origin[0]) if k == 0 else owner[k]
        return copy_to(z_out.at[p * 3 + k], z_in.at[p * 4 + slot], rzs.at[p * 3 + k],
                       rzr.at[p * 4 + slot], index(target, x, core))

    def sum_came(p, slot):
        copy_to(z_out.at[0], z_in.at[p * 4 + slot], rzs.at[0], rzr.at[p * 4 + slot], across).wait_recv()

    def onward(i):
        back_x(i).wait_recv()

        @pl.when(back_sends)
        def _():
            back_z(i).start()

    def compute(s):
        if s >= 2:
            sum_core(s - 2).wait_send()
        cols = pl.ds(pl.multiple_of(owner[s % 4] * wide, wide), wide)
        for j, k in enumerate(PASSES[s // 4]):
            left = cot_ref if k == 3 else acted_ref

            def term(i, carry, k=k, j=j, left=left):
                t = pl.ds(pl.multiple_of(i * wide_tile, wide_tile), wide_tile)
                if k == 3:
                    right = gated_ref[:, t]
                elif k == 1:
                    right = hg_ref[:, t]
                else:
                    right = near[x if k == 0 else 1 - x, :, t]
                p = lax.dot_general(left[:, cols], right, TN, preferred_element_type=F32)
                for xx in range(2):
                    lo = p[2 * xx * share:(2 * xx + 1) * share]
                    hi = p[(2 * xx + 1) * share:(2 * xx + 2) * share]
                    keep[s % 2, xx, j, :, t] = jnp.where(core == 0, lo, hi)
                    give[s % 2, xx, j, :, t] = jnp.where(core == 0, hi, lo)
                return carry

            lax.fori_loop(0, hid // wide_tile, term, 0)
        if s >= 2:
            pl.semaphore_wait(free, 1)
        sum_core(s).start()

    def to_across(s):
        sum_core(s).wait_recv()

        def add(j, carry):
            x_out[s, j] = (keep[s % 2, 1 - x, j] + got[s % 2, 1 - x, j]).astype(BF16)
            sums[terms(s, j), :] = keep[s % 2, x, j] + got[s % 2, x, j]
            return carry

        lax.fori_loop(0, 2, add, 0)
        if s != 3:
            sum_x(s).start()
        if s < 6:
            pl.semaphore_signal(free, inc=1, device_id={"seq": other}, device_id_type=MESH)

    def to_z(s):
        p, k = s // 4, s % 4
        sum_x(s).wait_recv()

        def plain():
            for j in range(2):
                z_out[p * 3 + k, j] = (sums[terms(s, j), :] + x_in[s, j].astype(F32)).astype(BF16)

        if k == 1:
            pl.when(jnp.logical_not(inside))(plain)

            @pl.when(inside)
            def _():
                sum_came(p, 3)
                for j in range(2):
                    z_out[p * 3 + k, j] = (
                        sums[terms(s, j), :] + x_in[s, j].astype(F32) + z_in[p * 4 + 3, j].astype(F32)
                    ).astype(BF16)
        else:
            plain()
        sum_z(s).start()

    def total(p):
        s = 4 * p + 3
        sum_x(s).wait_recv()
        sum_came(p, 2)
        sum_came(p, 1)
        for j in range(2):
            own = sums[terms(s, j), :] + x_in[s, j].astype(F32)
            for slot in (1, 2):
                own = own + z_in[p * 4 + slot, j].astype(F32)
            grads_ref[PASSES[p][j]] = own * scale

        @pl.when(inside)
        def _():
            sum_came(p, 0)
            for j in range(2):
                t = PASSES[p][j]
                grads_ref[t] = grads_ref[t] + z_in[p * 4, j].astype(F32) * scale

    span = 512

    def project(i, carry):
        def span_part(j, c):
            t = pl.ds(pl.multiple_of(j * span, span), span)
            p = lax.dot_general(gated_ref[rows(i), :], w_buf[3, t, :], NT, preferred_element_type=F32)
            o_buf[rows(i), t] = (x_ref[rows(i), t].astype(F32) + p).astype(BF16)
            return c

        lax.fori_loop(0, chans // span, span_part, 0)
        return carry

    def spread(i, carry):
        def span_part(j, c):
            t = pl.ds(pl.multiple_of(j * span, span), span)
            p = lax.dot_general(hg_ref[rows(i), :], w_buf[2, t, :], NT, preferred_element_type=F32)
            p += lax.dot_general(near[x, rows(i), :], w_buf[0, t, :], NT, preferred_element_type=F32)
            p += lax.dot_general(near[1 - x, rows(i), :], w_buf[1, t, :], NT, preferred_element_type=F32)
            slope = gelu_parts(x_ref[rows(i), t].astype(F32))[1]
            g_buf[rows(i), t] = (cot_ref[rows(i), t].astype(F32) + p * slope).astype(BF16)
            return c

        lax.fori_loop(0, chans // span, span_part, 0)
        return carry

    for load in loads:
        load.wait()
    z_begin(0)
    x_copy(0, 3).start()
    own_core().start()
    x_copy(1, 3).start()
    x_copy(2, 3).start()
    x_copy(3, 3).start()
    x_load.wait()
    steps = m // tile
    lax.fori_loop(0, steps // 2, act, 0)
    take_x(0, 3)
    z_begin(1)
    lax.fori_loop(steps // 2, steps, act, 0)
    take_z(0, 0)
    take_far(0, True)
    take_z(0, 1)
    x_came(1, 3)
    core_copy(1, 7).start()
    x_came(3, 3)
    take_y(0, 7)
    take_x(1, 0)
    take_z(1, 0)
    take_y(0, 0)
    take_far(1, True)
    z_begin(2)
    z_begin(3)
    z_begin(4)
    take_far(0, False)
    take_x(1, 1)
    take_z(1, 1)
    take_y(0, 1)
    take_far(1, False)
    take_x(1, 2)
    take_y(0, 2)
    take_z_early(2, 0)
    take_y(0, 4)
    take_x(1, 4)
    take_y(0, 5)
    take_x(1, 5)
    take_z_early(2, 1)
    take_y(0, 6)
    own_core_came()
    core_came(0)
    take_far(2, True)
    lax.fori_loop(0, 2, far_part, 0)
    take_x(1, 6)
    y_copy(2, 0, group).start()
    y_copy(2, 1, group).start()
    take_x(2, 3)
    take_y(1, 4)
    take_y(1, 5)
    take_x(2, 0)
    take_y(1, 6)
    take_x(2, 1)
    take_far(3, True)
    take_y(1, 0)
    take_y(1, 1)
    take_y(1, 2)
    y_copy(3, 7, group).start()
    core_came(1)
    take_far(4, True)
    lax.fori_loop(0, 2, near_part, 0)
    combine(0)
    lax.fori_loop(2, CHUNKS, near_part, 0)
    lax.fori_loop(2, CHUNKS, far_part, 0)
    take_far(2, False)
    take_z(3, 0)
    combine(1)
    take_x(2, 2)
    take_z(3, 1)
    take_z(4, 0)
    for j in (0, 1, 7, 4):
        take_y(2, j)
    combine(2)
    take_z(4, 1)
    for j in (5, 2, 6):
        take_y(2, j)
    combine(3)
    take_far(3, False)
    take_far(4, False)
    for j in (7, 0, 1, 4):
        take_y(3, j)
    combine(4)
    for j in (5, 2, 6):
        take_y(3, j)
    cot_load.wait()
    core_came(2)
    core_came(3)
    middle(0)
    combine(5)
    middle(1)
    combine(6)
    middle(2)
    combine(7)
    middle(3)
    for i in range(HALO):
        finish(i)

    @pl.when(jnp.logical_not(back_takes))
    def _():
        near[1] = jnp.zeros((m, hid), BF16)

    project(0, 0)
    compute(0)
    onward(0)
    project(1, 0)
    onward(1)
    compute(1)
    to_across(0)
    onward(2)
    compute(2)
    onward(3)
    to_across(1)
    compute(3)
    onward(4)
    to_across(2)
    project(2, 0)
    project(3, 0)
    onward(5)
    to_across(3)
    onward(6)
    onward(7)

    @pl.when(back_takes)
    def _():
        for i in range(HALO):
            back_z(i).wait_recv()

    compute(4)
    to_z(0)
    compute(5)
    to_across(4)
    to_z(1)
    compute(6)
    to_across(5)
    to_z(2)
    compute(7)
    to_across(6)
    sum_x(3).start()
    to_across(7)
    spread(0, 0)
    to_z(4)
    spread(1, 0)
    spread(2, 0)
    to_z(5)
    to_z(6)
    spread(3, 0)
    total(0)
    total(1)
    own_core().wait_send()
    for q in range(5):
        for d in range(2):
            z_copy(q, d).wait_send()

    @pl.when(inside)
    def _():
        for q in range(5):
            z_copy(q, 2).wait_send()
            z_onward(q).wait_send()

    for p, j in x_sent:
        x_copy(p, j).wait_send()
    for p in range(4):
        for j in swapped:
            if (p, j) != (1, 7):
                y_copy(p, j, group).wait_send()
            core_copy(p, j).wait_send()
    for i in range(HALO):
        halo_x(i).wait_send()
        back_x(i).wait_send()

    @pl.when(sends)
    def _():
        for i in range(HALO):
            halo_z(i).wait_send()

    @pl.when(back_sends)
    def _():
        for i in range(HALO):
            back_z(i).wait_send()

    sum_core(6).wait_send()
    sum_core(7).wait_send()
    for s in range(8):
        sum_x(s).wait_send()
        if s % 4 < 3:
            sum_z(s).wait_send()


def block(scale, conv_weight, proj_weight, flat, cot):
    share, hid = proj_weight.shape
    m, chans = flat.shape
    dma = pltpu.SemaphoreType.DMA
    pair = (2, 2, share, hid)
    halo = pltpu.VMEM((m, hid), BF16)
    wide = pltpu.VMEM((m, chans), BF16)
    return pl.pallas_call(
        functools.partial(block_kernel, scale),
        out_shape=(
            pltpu.VMEM((4, share, hid), F32), pltpu.VMEM((m, chans), BF16), pltpu.VMEM((m, chans), BF16),
        ),
        in_specs=[HBM] * 4,
        out_specs=(VMEM, VMEM, VMEM),
        scratch_shapes=[pltpu.VMEM((4, chans, hid), BF16), wide, wide, wide]
        + [halo] * 4 + [pltpu.VMEM((2 * m, hid), F32)] + [halo] * 2
        + [pltpu.VMEM((2, m, hid), BF16)]
        + [pltpu.VMEM((2,) + pair, F32)] * 3
        + [pltpu.VMEM((8, 2, share, hid), BF16)] * 2
        + [pltpu.VMEM((n, 2, share, hid), BF16) for n in (6, 8)]
        + [dma((8,)), dma((5, 4)), dma((5, 4))] + [dma((4, 8))] * 6
        + [dma((1,))] * 2 + [dma((HALO,))] * 8 + [dma((8,))] * 4 + [dma((6,)), dma((8,))]
        + [pltpu.SemaphoreType.REGULAR],
        compiler_params=params(1, 54),
        name="block_step",
    )(conv_weight, proj_weight, flat, cot)


def deliver_kernel(grads, outputs_in, input_grad_in, outputs, input_grad, conv, proj, gone):
    parts = 2
    m = outputs_in.shape[0] // parts
    moves = [(grads.at[pl.ds(0, 3)], conv), (grads.at[3], proj)]
    for i in range(parts):
        r = pl.ds(i * m, m)
        moves.append((outputs_in.at[r, :], outputs.at[r, :]))
        moves.append((input_grad_in.at[r, :], input_grad.at[r, :]))
    stores = [pltpu.make_async_copy(s, d, gone.at[i]) for i, (s, d) in enumerate(moves)]
    for store in stores:
        store.start()
    for store in stores:
        store.wait()


def deliver(grads, outputs, input_grad):
    like = lambda shape, kind: jax.ShapeDtypeStruct(shape, kind)
    return pl.pallas_call(
        deliver_kernel,
        out_shape=(
            like(outputs.shape, BF16), like(input_grad.shape, BF16),
            like((3,) + grads.shape[1:], F32), like(grads.shape[1:], F32),
        ),
        in_specs=[VMEM] * 3,
        out_specs=(HBM,) * 4,
        scratch_shapes=[pltpu.SemaphoreType.DMA((6,))],
        compiler_params=pltpu.CompilerParams(vmem_limit_bytes=2 * 1024 * 1024),
        name="deliver",
    )(grads, outputs, input_grad)


def pair_shards(inputs, conv_weight, proj_weight, cotangent):
    batch, local_len, chans = inputs.shape
    scale = 1.0 / float(batch * L) ** 0.5
    rows = inputs.reshape(-1, chans)
    cot = cotangent.reshape(-1, chans)
    outputs, input_grad, conv, proj = deliver(*block(scale, conv_weight, proj_weight, rows, cot))
    return (
        outputs.reshape(batch, local_len, chans),
        input_grad.reshape(batch, local_len, chans),
        conv.transpose(1, 0, 2),
        proj,
    )


def solution(mesh):
    fast = mesh.shape["seq"] == SEQ
    return jax.shard_map(
        pair_shards if fast else shards,
        mesh=mesh,
        in_specs=(
            P("groups", "seq", None),
            P(None, "seq", None),
            P("seq", None),
            P("groups", "seq", None),
        ),
        out_specs=(
            P("groups", "seq", None),
            P("groups", "seq", None),
            P(("groups", "seq"), None, None),
            P(("groups", "seq"), None),
        ),
        check_vma=False,
    )
```

```python
import functools

import jax
import jax.numpy as jnp
from jax import lax
from jax.experimental import pallas as pl
from jax.experimental.pallas import tpu as pltpu
from jax.sharding import PartitionSpec as P

L = 8192


def from_behind(block, axis, distance):
    devices = range(lax.axis_size(axis))
    route = [(i - distance, i) for i in devices if i - distance in devices]
    return lax.ppermute(block, axis, route)


def gelu_grad(point, upstream):
    return jax.vjp(jax.nn.gelu, point)[1](upstream)[0]


def shards(inputs, conv_weight, proj_weight, cotangent):
    batch, local_len, chans = inputs.shape
    devices = lax.axis_size("seq")
    stride = devices // 8
    scale = 1.0 / float(batch * L) ** 0.5
    acted = jax.nn.gelu(inputs.astype(jnp.float32)).astype(jnp.bfloat16)
    conv_weight, proj_weight = (
        lax.all_gather(conv_weight, "seq", axis=1, tiled=True),
        lax.all_gather(proj_weight, "seq", axis=0, tiled=True),
    )
    hid = conv_weight.shape[2]
    acted_rows = acted.reshape(-1, chans)
    before = from_behind(acted, "seq", stride)
    after = from_behind(acted, "seq", -stride)
    hidden = jnp.dot(before.reshape(-1, chans), conv_weight[0], preferred_element_type=jnp.float32)
    hidden = hidden + jnp.dot(acted_rows, conv_weight[1], preferred_element_type=jnp.float32)
    hidden = hidden + jnp.dot(
        after.reshape(-1, chans), conv_weight[2], preferred_element_type=jnp.float32
    )
    gated = jax.nn.gelu(hidden).astype(jnp.bfloat16)
    outputs = (
        inputs.reshape(-1, chans).astype(jnp.float32)
        + jnp.dot(gated, proj_weight.T, preferred_element_type=jnp.float32)
    ).astype(jnp.bfloat16)
    cot_rows = cotangent.reshape(-1, chans)
    gated_grad = jnp.dot(cot_rows, proj_weight, preferred_element_type=jnp.float32)
    hidden_grad = gelu_grad(hidden, gated_grad).astype(jnp.bfloat16)
    grad_blocks = hidden_grad.reshape(batch, local_len, hid)
    grad_later = from_behind(grad_blocks, "seq", -stride).reshape(-1, hid)
    grad_earlier = from_behind(grad_blocks, "seq", stride).reshape(-1, hid)
    acted_grad = jnp.dot(grad_later, conv_weight[0].T, preferred_element_type=jnp.float32)
    acted_grad = acted_grad + jnp.dot(
        hidden_grad, conv_weight[1].T, preferred_element_type=jnp.float32
    )
    acted_grad = acted_grad + jnp.dot(
        grad_earlier, conv_weight[2].T, preferred_element_type=jnp.float32
    )
    input_grad = (
        cot_rows.astype(jnp.float32)
        + gelu_grad(inputs.reshape(-1, chans).astype(jnp.float32), acted_grad)
    ).astype(jnp.bfloat16)
    tap_grads = (grad_later, hidden_grad, grad_earlier)
    share = chans // devices
    local_terms = [
        jnp.dot(acted_rows.T, piece, preferred_element_type=jnp.float32) for piece in tap_grads
    ]
    local_terms.append(jnp.dot(cot_rows.T, gated, preferred_element_type=jnp.float32))
    stacked = jnp.stack(local_terms, axis=1)
    received = lax.all_to_all(stacked, "seq", split_axis=0, concat_axis=0, tiled=True)
    summed = jnp.sum(received.reshape(devices, share, 4, received.shape[2]), axis=0)
    conv_sum = summed[:, 0:3, :]
    proj_sum = summed[:, 3, :]
    return (
        outputs.reshape(batch, local_len, chans),
        input_grad.reshape(batch, local_len, chans),
        conv_sum * scale,
        proj_sum * scale,
    )


F32 = jnp.float32
BF16 = jnp.bfloat16
MESH = pl.DeviceIdType.MESH
VMEM = pl.BlockSpec(memory_space=pltpu.VMEM)
HBM = pl.BlockSpec(memory_space=pl.ANY)
SEQ = 16
CHUNKS = 4
HALO = 8
COEF = 0.7978845608028654
CUBE = 0.044715


def place():
    s = lax.axis_index("seq")
    return s // 4, (s // 2) % 2, s % 2


def index(z, x, core):
    return (z * 2 + x) * 2 + core


def copy_to(src, dst, send, recv, target):
    return pltpu.make_async_remote_copy(
        src_ref=src, dst_ref=dst, send_sem=send, recv_sem=recv,
        device_id={"seq": target}, device_id_type=MESH,
    )


def gelu_parts(v):
    t = jnp.tanh(COEF * (v + CUBE * v * v * v))
    half = 0.5 * (1.0 + t)
    return half * v, half + (0.5 * COEF) * v * (1.0 - t * t) * (1.0 + (3.0 * CUBE) * v * v)


def params(cid, mib=56):
    return pltpu.CompilerParams(
        collective_id=cid, has_side_effects=True, vmem_limit_bytes=mib * 1024 * 1024
    )


PASSES = ((1, 3), (0, 2))
NT = (((1,), (1,)), ((), ()))
TN = (((0,), (0,)), ((), ()))


def block_kernel(scale, conv_hbm, proj_hbm, x_hbm, cot_hbm, grads_ref, o_buf, g_buf,
                 w_buf, x_ref, cot_ref, acted_ref, out_a, in_a, out_s, in_s, sums, gated_ref, hg_ref,
                 near, give, keep, got, x_out, x_in, z_out, z_in, own_sem,
                 zs, zr, xs, xr, ys, yr, cs, cr, os, orv, hzs, hzr, hxs, hxr,
                 bzs, bzr, bxs, bxr, rcs, rcr, rxs, rxr, rzs, rzr, free):
    z, x, core = place()
    group = lax.axis_index("groups")
    me = lax.axis_index("seq")
    share = proj_hbm.shape[0]
    across = index(z, 1 - x, core)
    other = index(z, x, 1 - core)
    origin = (z + 1 - 2 * lax.rem(z, 2), 2 - z // 2, 3 - 3 * (z // 2), z)
    up = x == 1
    sends = jnp.logical_or(jnp.logical_and(up, z < 3), jnp.logical_and(x == 0, z > 0))
    takes = jnp.logical_or(jnp.logical_and(up, z > 0), jnp.logical_and(x == 0, z < 3))
    ahead = index(lax.rem(z + (2 * x - 1) + 4, 4), x, core)

    mine = pl.ds(pl.multiple_of(me * share, share), share)
    loads = [
        pltpu.make_async_copy(conv_hbm.at[tap], w_buf.at[slot, mine, :], own_sem.at[slot])
        for slot, tap in enumerate((0, 2, 1))
    ]
    loads.append(pltpu.make_async_copy(proj_hbm, w_buf.at[3, mine, :], own_sem.at[3]))
    x_load = pltpu.make_async_copy(x_hbm, x_ref, own_sem.at[4])
    cot_load = pltpu.make_async_copy(cot_hbm, cot_ref, own_sem.at[5])
    for load in loads:
        load.start()
    x_load.start()
    cot_load.start()
    barrier = pltpu.get_barrier_semaphore()
    inside = jnp.logical_or(z == 1, z == 2)
    for target in (index(origin[0], x, core), index(origin[1], x, core), across, other):
        pl.semaphore_signal(barrier, inc=1, device_id={"seq": target}, device_id_type=MESH)

    @pl.when(inside)
    def _():
        pl.semaphore_signal(
            barrier, inc=1, device_id={"seq": index(origin[2], x, core)}, device_id_type=MESH
        )

    pl.semaphore_signal(
        barrier, inc=1, device_id={"groups": 1 - group, "seq": me}, device_id_type=MESH
    )
    pl.semaphore_wait(barrier, jnp.where(inside, 6, 5))

    slots = (1 - x, x, 2, 3)
    part = sums.at[pl.ds(0, acted_ref.shape[0]), :]
    gg = sums.at[pl.ds(acted_ref.shape[0], acted_ref.shape[0]), :]
    half = share // 2

    def piece(p, j, xx, start, size):
        begin = pl.multiple_of(index(origin[j], xx, core) * share + start, 16)
        return w_buf.at[slots[p], pl.ds(begin, size), :]

    def plane(p, j, xx):
        return piece(p, j, xx, group * half, half)

    def z_piece(q, j):
        return plane((0, 0, 2, 3, 3)[q], j, 1 - x if q in (1, 4) else x)

    def z_copy(q, d):
        place_ = z_piece(q, 3)
        return copy_to(place_, place_, zs.at[q, d], zr.at[q, z], index(origin[d], x, core))

    def z_onward(q):
        place_ = z_piece(q, 2)
        return copy_to(place_, place_, zs.at[q, 3], zr.at[q, origin[2]], index(origin[0], x, core))

    def z_came(q, j):
        place_ = z_piece(q, j)
        copy_to(place_, place_, zs.at[q, 0], zr.at[q, origin[j]], across).wait_recv()
    def z_begin(q):
        z_copy(q, 0).start()
        z_copy(q, 1).start()

        @pl.when(inside)
        def _():
            z_copy(q, 2).start()

    def x_copy(p, j):
        if (p, j) == (1, 3):
            place_ = piece(0, 3, x, 0, share)
        else:
            place_ = plane(1 - p if p < 2 else p, j % 4, x if j < 4 else 1 - x)
        return copy_to(place_, place_, xs.at[p, j], xr.at[p, j], across)

    def x_came(p, j):
        if (p, j) == (1, 3):
            place_ = piece(1, 3, 1 - x, 0, share)
        else:
            place_ = plane(p, j % 4, 1 - x if j < 4 else x)
        copy_to(place_, place_, xs.at[p, j], xr.at[p, j], across).wait_recv()

    def column(j):
        return j % 4, (x if j < 4 else 1 - x)

    def y_copy(p, j, whose):
        place_ = piece(p, *column(j), whose * half, half)
        return pltpu.make_async_remote_copy(
            src_ref=place_, dst_ref=place_, send_sem=ys.at[p, j], recv_sem=yr.at[p, j],
            device_id={"groups": 1 - group, "seq": me}, device_id_type=MESH,
        )

    def core_copy(p, j):
        place_ = piece(p, *column(j), 0, share)
        return copy_to(place_, place_, cs.at[p, j], cr.at[p, j], other)

    def own_core():
        place_ = w_buf.at[:, mine, :]
        return copy_to(place_, place_, os.at[0], orv.at[0], other)

    def own_core_came():
        start = pl.multiple_of(other * share, 16)
        place_ = w_buf.at[:, pl.ds(start, share), :]
        copy_to(place_, place_, os.at[0], orv.at[0], other).wait_recv()

    def take_z(q, j):
        z_came(q, j)
        k = j + 4 if q in (1, 4) else j
        y_copy((0, 0, 2, 3, 3)[q], k, group).start()
        if q < 3:
            x_copy(1 if q < 2 else 2, k).start()

    def take_far(q, here):
        @pl.when(inside if here else jnp.logical_not(inside))
        def _():
            z_came(q, 2)
            if here:
                z_onward(q).start()
            k = 6 if q in (1, 4) else 2
            if q < 3:
                x_copy(1 if q < 2 else 2, k).start()
            y_copy((0, 0, 2, 3, 3)[q], k, group).start()

    def take_z_early(q, j):
        z_came(q, j)
        x_copy(q, j).start()

    def take_x(p, j):
        x_came(p, j)
        y_copy(p, j + 4 if j < 4 else j - 4, group).start()

    def take_y(p, j):
        y_copy(p, j, 1 - group).wait_recv()
        core_copy(p, j).start()

    def core_came(p):
        for j in swapped:
            place_ = w_buf.at[
                slots[p],
                pl.ds(pl.multiple_of(index(origin[j % 4], x if j < 4 else 1 - x, 1 - core) * share, 16), share),
                :,
            ]
            copy_to(place_, place_, cs.at[p, j], cr.at[p, j], other).wait_recv()

    swapped = (0, 1, 2, 4, 5, 6, 7)
    x_sent = ((0, 3),) + tuple((1, j) for j in range(7)) + tuple((2, j) for j in range(4)) + ((3, 3),)
    m = acted_ref.shape[0]
    n = m // CHUNKS
    h = m // HALO

    def rows(i):
        return pl.ds(pl.multiple_of(i * n, n), n)

    def part_rows(i):
        return pl.ds(pl.multiple_of(i * h, h), h)

    def halo_z(i):
        r = part_rows(i)
        return copy_to(out_a.at[r, :], in_a.at[r, :], hzs.at[i], hzr.at[i], ahead)

    def halo_x(i):
        r = part_rows(i)
        return copy_to(out_s.at[r, :], in_s.at[r, :], hxs.at[i], hxr.at[i], across)

    tile = 64

    def act(i, carry):
        r = pl.ds(pl.multiple_of(i * tile, tile), tile)
        v = x_ref[r, :].astype(F32)
        t = jnp.tanh(COEF * (v + CUBE * v * v * v))
        acted_ref[r, :] = (0.5 * v * (1.0 + t)).astype(BF16)
        return carry

    def far_part(i, carry):
        out_a[rows(i), :] = jnp.dot(
            acted_ref[rows(i), :], w_buf[1 - x], preferred_element_type=F32
        ).astype(BF16)

        @pl.when(sends)
        def _():
            for k in range(HALO // CHUNKS):
                halo_z(i * (HALO // CHUNKS) + k).start()
        return carry

    def near_part(i, carry):
        part[rows(i), :] = jnp.dot(acted_ref[rows(i), :], w_buf[x], preferred_element_type=F32)
        return carry

    def combine(i):
        r = part_rows(i)

        @pl.when(takes)
        def _():
            halo_z(i).wait_recv()
            part[r, :] = part[r, :] + in_a[r, :].astype(F32)
        out_s[r, :] = part[r, :].astype(BF16)
        halo_x(i).start()

    def middle(i):
        part[rows(i), :] = jnp.dot(acted_ref[rows(i), :], w_buf[2], preferred_element_type=F32)
        gg[rows(i), :] = jnp.dot(cot_ref[rows(i), :], w_buf[3], preferred_element_type=F32)

    def finish(i):
        r = part_rows(i)
        halo_x(i).wait_recv()
        hidden = part[r, :] + in_s[r, :].astype(F32)
        value, slope = gelu_parts(hidden)
        gated_ref[r, :] = value.astype(BF16)
        hg_ref[r, :] = (gg[r, :] * slope).astype(BF16)
        back_x(i).start()

    wide = 4 * share
    wide_tile = 256
    hid = hg_ref.shape[1]
    chans = acted_ref.shape[1]
    even = x == 0
    back_sends = jnp.logical_or(jnp.logical_and(even, z < 3), jnp.logical_and(x == 1, z > 0))
    back_takes = jnp.logical_or(jnp.logical_and(even, z > 0), jnp.logical_and(x == 1, z < 3))
    back_ahead = index(lax.rem(z + (1 - 2 * x) + 4, 4), x, core)
    owner = (
        jnp.where(inside, origin[1], origin[2]), jnp.where(inside, origin[2], origin[1]), origin[0], z
    )

    def back_x(i):
        r = part_rows(i)
        return copy_to(hg_ref.at[r, :], near.at[0, r, :], bxs.at[i], bxr.at[i], across)

    def back_z(i):
        r = part_rows(i)
        return copy_to(near.at[0, r, :], near.at[1, r, :], bzs.at[i], bzr.at[i], back_ahead)

    def terms(s, j):
        return pl.ds(pl.multiple_of((2 * s + j) * share, share), share)

    def sum_core(s):
        return copy_to(give.at[s % 2], got.at[s % 2], rcs.at[s], rcr.at[s], other)

    def sum_x(s):
        return copy_to(x_out.at[s], x_in.at[s], rxs.at[s], rxr.at[s], across)

    def sum_z(s):
        p, k = s // 4, s % 4
        slot = jnp.where(inside, 0, 3) if k == 0 else k
        target = jnp.where(inside, origin[1], origin[0]) if k == 0 else owner[k]
        return copy_to(z_out.at[p * 3 + k], z_in.at[p * 4 + slot], rzs.at[p * 3 + k],
                       rzr.at[p * 4 + slot], index(target, x, core))

    def sum_came(p, slot):
        copy_to(z_out.at[0], z_in.at[p * 4 + slot], rzs.at[0], rzr.at[p * 4 + slot], across).wait_recv()

    def onward(i):
        back_x(i).wait_recv()

        @pl.when(back_sends)
        def _():
            back_z(i).start()

    def compute(s):
        if s >= 2:
            sum_core(s - 2).wait_send()
        cols = pl.ds(pl.multiple_of(owner[s % 4] * wide, wide), wide)
        for j, k in enumerate(PASSES[s // 4]):
            left = cot_ref if k == 3 else acted_ref

            def term(i, carry, k=k, j=j, left=left):
                t = pl.ds(pl.multiple_of(i * wide_tile, wide_tile), wide_tile)
                if k == 3:
                    right = gated_ref[:, t]
                elif k == 1:
                    right = hg_ref[:, t]
                else:
                    right = near[x if k == 0 else 1 - x, :, t]
                p = lax.dot_general(left[:, cols], right, TN, preferred_element_type=F32)
                for xx in range(2):
                    lo = p[2 * xx * share:(2 * xx + 1) * share]
                    hi = p[(2 * xx + 1) * share:(2 * xx + 2) * share]
                    keep[s % 2, xx, j, :, t] = jnp.where(core == 0, lo, hi)
                    give[s % 2, xx, j, :, t] = jnp.where(core == 0, hi, lo)
                return carry

            lax.fori_loop(0, hid // wide_tile, term, 0)
        if s >= 2:
            pl.semaphore_wait(free, 1)
        sum_core(s).start()

    def to_across(s):
        sum_core(s).wait_recv()

        def add(j, carry):
            x_out[s, j] = (keep[s % 2, 1 - x, j] + got[s % 2, 1 - x, j]).astype(BF16)
            sums[terms(s, j), :] = keep[s % 2, x, j] + got[s % 2, x, j]
            return carry

        lax.fori_loop(0, 2, add, 0)
        if s != 3:
            sum_x(s).start()
        if s < 6:
            pl.semaphore_signal(free, inc=1, device_id={"seq": other}, device_id_type=MESH)

    def to_z(s):
        p, k = s // 4, s % 4
        sum_x(s).wait_recv()

        def plain():
            for j in range(2):
                z_out[p * 3 + k, j] = (sums[terms(s, j), :] + x_in[s, j].astype(F32)).astype(BF16)

        if k == 1:
            pl.when(jnp.logical_not(inside))(plain)

            @pl.when(inside)
            def _():
                sum_came(p, 3)
                for j in range(2):
                    z_out[p * 3 + k, j] = (
                        sums[terms(s, j), :] + x_in[s, j].astype(F32) + z_in[p * 4 + 3, j].astype(F32)
                    ).astype(BF16)
        else:
            plain()
        sum_z(s).start()

    def total(p):
        s = 4 * p + 3
        sum_x(s).wait_recv()
        sum_came(p, 2)
        sum_came(p, 1)
        for j in range(2):
            own = sums[terms(s, j), :] + x_in[s, j].astype(F32)
            for slot in (1, 2):
                own = own + z_in[p * 4 + slot, j].astype(F32)
            grads_ref[PASSES[p][j]] = own * scale

        @pl.when(inside)
        def _():
            sum_came(p, 0)
            for j in range(2):
                t = PASSES[p][j]
                grads_ref[t] = grads_ref[t] + z_in[p * 4, j].astype(F32) * scale

    span = 512

    def project(i, carry):
        def span_part(j, c):
            t = pl.ds(pl.multiple_of(j * span, span), span)
            p = lax.dot_general(gated_ref[rows(i), :], w_buf[3, t, :], NT, preferred_element_type=F32)
            o_buf[rows(i), t] = (x_ref[rows(i), t].astype(F32) + p).astype(BF16)
            return c

        lax.fori_loop(0, chans // span, span_part, 0)
        return carry

    def spread(i, carry):
        def span_part(j, c):
            t = pl.ds(pl.multiple_of(j * span, span), span)
            p = lax.dot_general(hg_ref[rows(i), :], w_buf[2, t, :], NT, preferred_element_type=F32)
            p += lax.dot_general(near[x, rows(i), :], w_buf[0, t, :], NT, preferred_element_type=F32)
            p += lax.dot_general(near[1 - x, rows(i), :], w_buf[1, t, :], NT, preferred_element_type=F32)
            slope = gelu_parts(x_ref[rows(i), t].astype(F32))[1]
            g_buf[rows(i), t] = (cot_ref[rows(i), t].astype(F32) + p * slope).astype(BF16)
            return c

        lax.fori_loop(0, chans // span, span_part, 0)
        return carry

    for load in loads[:2]:
        load.wait()
    z_begin(0)
    x_copy(0, 3).start()
    x_copy(1, 3).start()
    for load in loads[2:]:
        load.wait()
    own_core().start()
    x_copy(2, 3).start()
    x_copy(3, 3).start()
    x_load.wait()
    steps = m // tile
    lax.fori_loop(0, steps // 2, act, 0)
    take_x(0, 3)
    z_begin(1)
    lax.fori_loop(steps // 2, steps, act, 0)
    take_z(0, 0)
    take_far(0, True)
    take_z(0, 1)
    x_came(1, 3)
    core_copy(1, 7).start()
    x_came(3, 3)
    take_y(0, 7)
    take_x(1, 0)
    take_z(1, 0)
    take_y(0, 0)
    take_far(1, True)
    z_begin(2)
    z_begin(3)
    z_begin(4)
    take_far(0, False)
    take_x(1, 1)
    take_z(1, 1)
    take_y(0, 1)
    take_far(1, False)
    take_x(1, 2)
    take_y(0, 2)
    take_z_early(2, 0)
    take_y(0, 4)
    take_x(1, 4)
    take_y(0, 5)
    take_x(1, 5)
    take_z_early(2, 1)
    take_y(0, 6)
    own_core_came()
    core_came(0)
    take_far(2, True)
    lax.fori_loop(0, 2, far_part, 0)
    take_x(1, 6)
    y_copy(2, 0, group).start()
    y_copy(2, 1, group).start()
    take_x(2, 3)
    take_y(1, 4)
    take_y(1, 5)
    take_x(2, 0)
    take_y(1, 6)
    take_x(2, 1)
    take_far(3, True)
    take_y(1, 0)
    take_y(1, 1)
    take_y(1, 2)
    y_copy(3, 7, group).start()
    core_came(1)
    take_far(4, True)
    lax.fori_loop(0, 2, near_part, 0)
    combine(0)
    lax.fori_loop(2, CHUNKS, near_part, 0)
    lax.fori_loop(2, CHUNKS, far_part, 0)
    take_far(2, False)
    take_z(3, 0)
    combine(1)
    take_x(2, 2)
    take_z(3, 1)
    take_z(4, 0)
    for j in (0, 1, 7, 4):
        take_y(2, j)
    combine(2)
    take_z(4, 1)
    for j in (5, 2, 6):
        take_y(2, j)
    combine(3)
    take_far(3, False)
    take_far(4, False)
    for j in (7, 0, 1, 4):
        take_y(3, j)
    combine(4)
    for j in (5, 2, 6):
        take_y(3, j)
    cot_load.wait()
    core_came(2)
    core_came(3)
    middle(0)
    combine(5)
    middle(1)
    combine(6)
    middle(2)
    combine(7)
    middle(3)
    for i in range(HALO):
        finish(i)

    @pl.when(jnp.logical_not(back_takes))
    def _():
        near[1] = jnp.zeros((m, hid), BF16)

    project(0, 0)
    compute(0)
    onward(0)
    project(1, 0)
    onward(1)
    compute(1)
    to_across(0)
    onward(2)
    compute(2)
    onward(3)
    to_across(1)
    compute(3)
    onward(4)
    to_across(2)
    project(2, 0)
    project(3, 0)
    onward(5)
    to_across(3)
    onward(6)
    onward(7)

    @pl.when(back_takes)
    def _():
        for i in range(HALO):
            back_z(i).wait_recv()

    compute(4)
    to_z(0)
    compute(5)
    to_across(4)
    to_z(1)
    compute(6)
    to_across(5)
    to_z(2)
    compute(7)
    to_across(6)
    sum_x(3).start()
    to_across(7)
    to_z(4)
    spread(0, 0)
    spread(1, 0)
    to_z(5)
    spread(2, 0)
    to_z(6)
    spread(3, 0)
    total(0)
    total(1)
    own_core().wait_send()
    for q in range(5):
        for d in range(2):
            z_copy(q, d).wait_send()

    @pl.when(inside)
    def _():
        for q in range(5):
            z_copy(q, 2).wait_send()
            z_onward(q).wait_send()

    for p, j in x_sent:
        x_copy(p, j).wait_send()
    for p in range(4):
        for j in swapped:
            if (p, j) != (1, 7):
                y_copy(p, j, group).wait_send()
            core_copy(p, j).wait_send()
    for i in range(HALO):
        halo_x(i).wait_send()
        back_x(i).wait_send()

    @pl.when(sends)
    def _():
        for i in range(HALO):
            halo_z(i).wait_send()

    @pl.when(back_sends)
    def _():
        for i in range(HALO):
            back_z(i).wait_send()

    sum_core(6).wait_send()
    sum_core(7).wait_send()
    for s in range(8):
        sum_x(s).wait_send()
        if s % 4 < 3:
            sum_z(s).wait_send()


def block(scale, conv_weight, proj_weight, flat, cot):
    share, hid = proj_weight.shape
    m, chans = flat.shape
    dma = pltpu.SemaphoreType.DMA
    pair = (2, 2, share, hid)
    halo = pltpu.VMEM((m, hid), BF16)
    wide = pltpu.VMEM((m, chans), BF16)
    return pl.pallas_call(
        functools.partial(block_kernel, scale),
        out_shape=(
            pltpu.VMEM((4, share, hid), F32), pltpu.VMEM((m, chans), BF16), pltpu.VMEM((m, chans), BF16),
        ),
        in_specs=[HBM] * 4,
        out_specs=(VMEM, VMEM, VMEM),
        scratch_shapes=[pltpu.VMEM((4, chans, hid), BF16), wide, wide, wide]
        + [halo] * 4 + [pltpu.VMEM((2 * m, hid), F32)] + [halo] * 2
        + [pltpu.VMEM((2, m, hid), BF16)]
        + [pltpu.VMEM((2,) + pair, F32)] * 3
        + [pltpu.VMEM((8, 2, share, hid), BF16)] * 2
        + [pltpu.VMEM((n, 2, share, hid), BF16) for n in (6, 8)]
        + [dma((8,)), dma((5, 4)), dma((5, 4))] + [dma((4, 8))] * 6
        + [dma((1,))] * 2 + [dma((HALO,))] * 8 + [dma((8,))] * 4 + [dma((6,)), dma((8,))]
        + [pltpu.SemaphoreType.REGULAR],
        compiler_params=params(1, 54),
        name="block_step",
    )(conv_weight, proj_weight, flat, cot)


def deliver_kernel(grads, outputs_in, input_grad_in, outputs, input_grad, conv, proj, gone):
    parts = 2
    m = outputs_in.shape[0] // parts
    moves = [(grads.at[pl.ds(0, 3)], conv), (grads.at[3], proj)]
    for i in range(parts):
        r = pl.ds(i * m, m)
        moves.append((outputs_in.at[r, :], outputs.at[r, :]))
        moves.append((input_grad_in.at[r, :], input_grad.at[r, :]))
    stores = [pltpu.make_async_copy(s, d, gone.at[i]) for i, (s, d) in enumerate(moves)]
    for store in stores:
        store.start()
    for store in stores:
        store.wait()


def deliver(grads, outputs, input_grad):
    like = lambda shape, kind: jax.ShapeDtypeStruct(shape, kind)
    return pl.pallas_call(
        deliver_kernel,
        out_shape=(
            like(outputs.shape, BF16), like(input_grad.shape, BF16),
            like((3,) + grads.shape[1:], F32), like(grads.shape[1:], F32),
        ),
        in_specs=[VMEM] * 3,
        out_specs=(HBM,) * 4,
        scratch_shapes=[pltpu.SemaphoreType.DMA((6,))],
        compiler_params=pltpu.CompilerParams(vmem_limit_bytes=2 * 1024 * 1024),
        name="deliver",
    )(grads, outputs, input_grad)


def pair_shards(inputs, conv_weight, proj_weight, cotangent):
    batch, local_len, chans = inputs.shape
    scale = 1.0 / float(batch * L) ** 0.5
    rows = inputs.reshape(-1, chans)
    cot = cotangent.reshape(-1, chans)
    outputs, input_grad, conv, proj = deliver(*block(scale, conv_weight, proj_weight, rows, cot))
    return (
        outputs.reshape(batch, local_len, chans),
        input_grad.reshape(batch, local_len, chans),
        conv.transpose(1, 0, 2),
        proj,
    )


def solution(mesh):
    fast = mesh.shape["seq"] == SEQ
    return jax.shard_map(
        pair_shards if fast else shards,
        mesh=mesh,
        in_specs=(
            P("groups", "seq", None),
            P(None, "seq", None),
            P("seq", None),
            P("groups", "seq", None),
        ),
        out_specs=(
            P("groups", "seq", None),
            P("groups", "seq", None),
            P(("groups", "seq"), None, None),
            P(("groups", "seq"), None),
        ),
        check_vma=False,
    )
```
